32 devices in a mesh: group: 4 (over y, x), leaf: 8 (over z, core).
Axes of the slice: x: 2, y: 2, z: 4, core: 2. Of those that a mesh axis runs over, the one named last changes fastest.
Arguments:
- points: bfloat16 [65536, 64], P(('group', 'leaf')), may hold values from -1.1953125 to 1.1953125
- ordering: int32 [32, 2048], P(('group', 'leaf')), may hold values from 0 to 2047, each once within a row
- iterate: float32 [65536, 128], P(('group', 'leaf')), may hold values from -6 to 6
- target: float32 [65536, 128], P(('group', 'leaf')), may hold values from -18 to 18
- step_size: float32 [128], replicated, may hold values from 0.1 to 0.5
- leaf_basis: bfloat16 [65536, 256], P(('group', 'leaf')), may hold values from -0.125 to 0.125
- transfer: bfloat16 [32, 256, 256], P(('group', 'leaf')), may hold values from -0.375 to 0.375
- leaf_skeleton: bfloat16 [32, 256, 64], P(('group', 'leaf')), may hold values from -0.8984375 to 0.8984375
- cluster_skeleton: bfloat16 [4, 256, 64], P('group'), may hold values from -1.1953125 to 1.1953125
- near_table: int32 [32, 8], P(('group', 'leaf')), may hold values from 0 to 1, as said below
- far_table: int32 [32, 8], P(('group', 'leaf')), may hold values from 0 to 1, as said below
- cluster_far: int32 [4, 4], P('group'), may hold values from 0 to 1, as said below
Outputs:
- updated: float32 [65536, 128], P(('group', 'leaf'))
The draws below stay inside these ranges and needn't reach their ends.
Inputs may be any that keep to these rules, and one draw needn't show every extreme that they name: `near_table`: entries 0 or 1; each leaf's own place is 1; a 1 stands only at places at most 3 away from the leaf's own place; each row has at most 7 ones, and some row exactly 7. `far_table`: entries 0 or 1, never 1 where near_table is 1. `cluster_far`: entries 0 or 1, zero on the diagonal. `ordering`: each row is a permutation.
All inputs are finite; a program needn't handle non-finite values.
Results may differ from the reference program's by a relative error of at most 0.0044.
Values may be sent and summed in bfloat16 or wider, within the bound.
No kernel may reach another device: no remote copies, remote signals or barrier semaphores. Data moves between devices by JAX's collectives and lax.ppermute only.
A program may use at most 128 MiB of HBM per device.

```python
import math
import jax
import jax.numpy as jnp
from jax import lax

DIM = 64
RANK = 256
NRHS = 128
LEAF = 2048
NEAR_MOST = 7
CLUSTER = 8
GROUPS = 4
LEAVES = 32
POINTS = 65536


def near_pattern(key):
    reach = (NEAR_MOST - 1) // 2
    leaf_ids = jnp.arange(LEAVES, dtype=jnp.int32)
    own_place = leaf_ids % CLUSTER
    places = jnp.arange(CLUSTER, dtype=jnp.int32)
    base_key = jax.random.fold_in(key, 11)
    coin_key, group_key, place_key = jax.random.split(base_key, 3)
    distance = jnp.abs(places[None, :] - own_place[:, None])
    within = (distance <= reach) & (distance > 0)
    coins = jax.random.randint(coin_key, (LEAVES, CLUSTER), 0, 2)
    busy_group = jax.random.randint(group_key, (), 0, GROUPS)
    busy_place = jax.random.randint(place_key, (), reach, CLUSTER - reach)
    busiest = busy_group * CLUSTER + busy_place
    coins = jnp.where((leaf_ids == busiest)[:, None], 1, coins)
    chosen = (distance == 0) | within & (coins > 0)
    return chosen.astype(jnp.int32)


def draw_near_table(key, part):
    return near_pattern(key)


def draw_far_table(key, part):
    nearby = near_pattern(key)
    dice_roll = jax.random.randint(jax.random.fold_in(key, 12), (LEAVES, CLUSTER), 0, 4)
    return ((nearby == 0) & (dice_roll > 0)).astype(jnp.int32)


def draw_cluster_far(key, part):
    dice_roll = jax.random.randint(jax.random.fold_in(key, 13), (GROUPS, GROUPS), 0, 3)
    ids = jnp.arange(GROUPS, dtype=jnp.int32)
    return ((dice_roll > 0) & (ids[:, None] != ids[None, :])).astype(jnp.int32)


def level_of(own_key, dims, shards, low, high):
    factor_of = 1.0
    for dim, shards_of in shards:
        heights = jax.random.uniform(jax.random.fold_in(jax.random.fold_in(own_key, 6), dim), (shards_of,), jnp.float32, low / len(shards), high / len(shards))
        factor_of = factor_of * jnp.repeat(jnp.exp(heights), dims[dim] // shards_of).reshape((-1,) + (1,) * (len(dims) - 1 - dim))
    return factor_of


def scatter_about(stream_key, dims, width, most, cuts=(), held_as=jnp.bfloat16):
    entries = width * jax.random.normal(stream_key, dims, jnp.float32)
    if cuts:
        entries = entries * level_of(stream_key, dims, cuts, -0.22, 0.18)
    return jnp.clip(entries, -most, most).astype(held_as)


def setup_inputs(seed: int = 0) -> dict:
    key_of = jax.random.split(jax.random.key(seed), 13)
    return {
        "points": scatter_about(key_of[0], (POINTS, DIM), 0.2, 1.1953125, ((0, 32),)),
        "ordering": jax.vmap(lambda own: jax.random.permutation(own, LEAF))(jax.random.split(key_of[1], LEAVES)).reshape((LEAVES, LEAF)).astype(jnp.int32),
        "iterate": scatter_about(key_of[2], (POINTS, NRHS), 1.0, 6.0, ((0, 32),), jnp.float32),
        "target": scatter_about(key_of[3], (POINTS, NRHS), 3.0, 18.0, ((0, 32),), jnp.float32),
        "step_size": jnp.clip(jnp.exp(jax.random.uniform(key_of[4], (NRHS,), jnp.float32, math.log(0.1), math.log(0.5))), 0.1, 0.5),
        "leaf_basis": scatter_about(key_of[5], (POINTS, RANK), LEAF ** -0.5, 0.125, ((0, 32),)),
        "transfer": scatter_about(key_of[6], (LEAVES, RANK, RANK), RANK ** -0.5, 0.375, ((0, 32),)),
        "leaf_skeleton": scatter_about(key_of[7], (LEAVES, RANK, DIM), 0.15, 0.8984375, ((0, 32),)),
        "cluster_skeleton": scatter_about(key_of[8], (GROUPS, RANK, DIM), 0.2, 1.1953125, ((0, 4),)),
        "near_table": draw_near_table(jax.random.fold_in(key_of[12], 71), 0),
        "far_table": draw_far_table(jax.random.fold_in(key_of[12], 71), 0),
        "cluster_far": draw_cluster_far(jax.random.fold_in(key_of[12], 71), 0),
    }


def kernel_tile(left, right):
    left_f = left.astype(jnp.float32)
    right_f = right.astype(jnp.float32)
    left_sq = jnp.sum(left_f * left_f, axis=1)
    right_sq = jnp.sum(right_f * right_f, axis=1)
    inner = lax.dot_general(left, right, (((1,), (1,)), ((), ())), preferred_element_type=jnp.float32)
    return jnp.exp(-(left_sq[:, None] + right_sq[None, :] - 2.0 * inner)).astype(jnp.bfloat16)


def reference(points, ordering, iterate, target, step_size, leaf_basis, transfer, leaf_skeleton, cluster_skeleton, near_table, far_table, cluster_far):
    cloud = points.reshape(LEAVES, LEAF, DIM)
    rounded = iterate.astype(jnp.bfloat16).reshape(LEAVES, LEAF, NRHS)
    basis = leaf_basis.reshape(LEAVES, LEAF, RANK)
    coeffs = lax.map(lambda operands: jnp.dot(operands[0].T, operands[1], preferred_element_type=jnp.float32), (basis, rounded)).astype(jnp.bfloat16)

    def near_leaf(leaf_id):
        first_leaf = (leaf_id // CLUSTER) * CLUSTER
        own_points = cloud[leaf_id]

        def visit(place, running):
            other = first_leaf + place

            def include(summed):
                return summed + jnp.dot(kernel_tile(own_points, cloud[other]), rounded[other], preferred_element_type=jnp.float32)
            return lax.cond(near_table[leaf_id, place] > 0, include, lambda summed: summed, running)
        return lax.fori_loop(0, CLUSTER, visit, jnp.zeros((LEAF, NRHS), jnp.float32))

    def far_leaf(leaf_id):
        first_leaf = (leaf_id // CLUSTER) * CLUSTER
        own_skeleton = leaf_skeleton[leaf_id]

        def visit(place, running):
            other = first_leaf + place

            def include(summed):
                return summed + jnp.dot(kernel_tile(own_skeleton, leaf_skeleton[other]), coeffs[other], preferred_element_type=jnp.float32)
            return lax.cond(far_table[leaf_id, place] > 0, include, lambda summed: summed, running)
        return lax.fori_loop(0, CLUSTER, visit, jnp.zeros((RANK, NRHS), jnp.float32))

    leaf_ids = jnp.arange(LEAVES, dtype=jnp.int32)
    near_sum = lax.map(near_leaf, leaf_ids)
    far_sum = lax.map(far_leaf, leaf_ids)
    upward_terms = lax.map(lambda operands: jnp.dot(operands[0].T, operands[1], preferred_element_type=jnp.float32), (transfer, coeffs))
    upper = jnp.sum(upward_terms.reshape(GROUPS, CLUSTER, RANK, NRHS), axis=1).astype(jnp.bfloat16)

    def cluster_row(group_id):
        def visit(other, running):
            def include(summed):
                return summed + jnp.dot(kernel_tile(cluster_skeleton[group_id], cluster_skeleton[other]), upper[other], preferred_element_type=jnp.float32)
            return lax.cond(cluster_far[group_id, other] > 0, include, lambda summed: summed, running)
        return lax.fori_loop(0, GROUPS, visit, jnp.zeros((RANK, NRHS), jnp.float32))

    lower = lax.map(cluster_row, jnp.arange(GROUPS, dtype=jnp.int32)).astype(jnp.bfloat16)
    parent = jnp.repeat(lower, CLUSTER, axis=0)
    local = (far_sum + lax.map(lambda operands: jnp.dot(operands[0], operands[1], preferred_element_type=jnp.float32), (transfer, parent))).astype(jnp.bfloat16)
    image = lax.map(lambda operands: jnp.dot(operands[0], operands[1], preferred_element_type=jnp.float32), (basis, local)) + near_sum
    sorted_target = jnp.take_along_axis(target.reshape(LEAVES, LEAF, NRHS), ordering[:, :, None].astype(jnp.int32), axis=1)
    updated = iterate.reshape(LEAVES, LEAF, NRHS) + step_size[None, None, :] * (sorted_target - image)
    return updated.reshape(POINTS, NRHS)
```

```python
import jax
import jax.numpy as jnp
from jax import lax
from jax.experimental import pallas as pl
from jax.experimental.pallas import tpu as pltpu
from jax.sharding import PartitionSpec as P

LANES = 128
COLS = 256
VMEM = pltpu.VMEM
SMEM = pltpu.SMEM
F32 = jnp.float32
BF16 = jnp.bfloat16


def contract(left, right, dims):
    return lax.dot_general(left, right, (dims, ((), ())), preferred_element_type=F32)


def matmul(left, right):
    return contract(left, right, ((1,), (0,)))


def call(kernel, outs, ins, scratch=(), flops=0, limit=40, name=None):
    single = not isinstance(outs, (list, tuple))
    shapes = [outs] if single else list(outs)
    results = pl.pallas_call(
        kernel,
        out_shape=shapes,
        in_specs=[pl.BlockSpec(memory_space=space) for _, space in ins],
        out_specs=[pl.BlockSpec(memory_space=VMEM)] * len(shapes),
        scratch_shapes=list(scratch),
        compiler_params=pltpu.CompilerParams(vmem_limit_bytes=limit << 20),
        cost_estimate=pl.CostEstimate(
            flops=flops, bytes_accessed=sum(a.size * a.dtype.itemsize for a, _ in ins), transcendentals=0
        ),
        name=name,
    )(*[a for a, _ in ins])
    return results[0] if single else results


def three_parts(value):
    high = value.astype(BF16).astype(F32)
    rest = value - high
    middle = rest.astype(BF16).astype(F32)
    return high, middle, rest - middle


def left_form(points):
    rows, dim = points.shape
    width = LANES
    spread = (
        lax.broadcasted_iota(jnp.int32, (dim, width), 0) == lax.broadcasted_iota(jnp.int32, (dim, width), 1)
    ).astype(BF16)
    padded = matmul(points, spread)
    parts = three_parts(-jnp.sum(padded * padded, axis=1, keepdims=True))
    lane = lax.broadcasted_iota(jnp.int32, (rows, width), 1)
    form = jnp.where((lane >= dim) & (lane < dim + 3), 1.0, padded)
    for k, part in enumerate(parts):
        form = jnp.where(lane == dim + 3 + k, part, form)
    return form.astype(BF16)


def doubled_transpose(points):
    dim = points.shape[1]
    two = (
        2
        * (
            lax.broadcasted_iota(jnp.int32, (dim, dim), 0) == lax.broadcasted_iota(jnp.int32, (dim, dim), 1)
        ).astype(F32)
    ).astype(BF16)
    return contract(two, points, ((1,), (1,))).astype(BF16)


def right_form(doubled):
    dim, width = doubled.shape
    wide = doubled.astype(F32)
    parts = three_parts(-0.25 * jnp.sum(wide * wide, axis=0, keepdims=True))
    row = lax.broadcasted_iota(jnp.int32, (LANES - dim, width), 0)
    below = jnp.where((row >= 3) & (row < 6), 1.0, 0.0)
    for k, part in enumerate(parts):
        below = jnp.where(row == k, part, below)
    return jnp.concatenate([doubled, below.astype(BF16)], axis=0)


def tile(left, right):
    return jnp.exp(matmul(left, right)).astype(BF16)


def pick(row, place):
    lane = lax.broadcasted_iota(jnp.int32, row.shape, 1)
    return jnp.sum(jnp.where(lane == place, row, 0.0))


def listed(row_ref, place):
    size = row_ref.shape[1]
    inside = (place >= 0) & (place < size)
    return inside & (row_ref[0, jnp.clip(place, 0, size - 1)] > 0)


class Plan:
    def __init__(self, points, iterate):
        self.n, self.dim = points.shape
        self.rhs = iterate.shape[1]
        self.half = self.n // 2
        self.blocks = self.half // LANES
        self.block_rows = self.half + self.blocks * self.dim


def add_half(plan, acc_ref, left_ref, left_rows, half_ref, form_ref, fresh):
    if fresh:
        for b in range(plan.blocks):
            rows = slice(plan.half + b * plan.dim, plan.half + (b + 1) * plan.dim)
            form_ref[:, b * LANES : (b + 1) * LANES] = right_form(half_ref[rows, :])
    left = left_ref[left_rows, :]
    total = acc_ref[...]
    for j in range(plan.half // COLS):
        cols = slice(j * COLS, (j + 1) * COLS)
        total = total + matmul(tile(left, form_ref[:, cols]), half_ref[cols, :])
    acc_ref[...] = total


def prepare(plan, near_row, iterate, points):
    size = near_row.shape[1]
    n, half, blocks, dim = plan.n, plan.half, plan.blocks, plan.dim
    flag_rows = 16

    def kernel(near_ref, iterate_ref, points_ref, pay_ref, local_ref):
        other = 1 - lax.rem(lax.axis_index("leaf"), 2)
        for h in range(2):
            pay_ref[h, 0:half, :] = iterate_ref[h * half : (h + 1) * half, :].astype(BF16)
            for b in range(blocks):
                first = h * half + b * LANES
                pay_ref[h, half + b * dim : half + (b + 1) * dim, :] = doubled_transpose(
                    points_ref[first : first + LANES, :]
                )
        step = 512
        for r in range(0, n, step):
            local_ref[r : r + step, :] = left_form(points_ref[r : r + step, :])
        local_ref[n : n + plan.block_rows, :] = pay_ref[other]
        lane = lax.broadcasted_iota(jnp.int32, (flag_rows, LANES), 1)
        row = jnp.zeros((flag_rows, LANES), F32)
        for k in range(size):
            row = jnp.where(lane == k, near_ref[0, k].astype(F32), row)
        local_ref[n + plan.block_rows :, :] = row.astype(BF16)

    return call(
        kernel,
        [
            jax.ShapeDtypeStruct((2, plan.block_rows, LANES), BF16),
            jax.ShapeDtypeStruct((n + plan.block_rows + flag_rows, LANES), BF16),
        ],
        [(near_row, SMEM), (iterate, VMEM), (points, VMEM)],
        flops=2 * n * dim * LANES * 2,
        name="prepare",
    )


def own_tile(plan, local, pay):
    def kernel(local_ref, pay_ref, acc_ref, form_ref):
        acc_ref[...] = jnp.zeros_like(acc_ref)
        for h in range(2):
            add_half(plan, acc_ref, local_ref, slice(0, plan.n), pay_ref.at[h], form_ref, True)

    return call(
        kernel,
        jax.ShapeDtypeStruct((plan.n, plan.rhs), F32),
        [(local, VMEM), (pay, VMEM)],
        scratch=[VMEM((LANES, plan.half), BF16)],
        flops=2 * plan.n * plan.n * 512,
        name="own_tile",
    )


def flags_of(plan, partner_ref):
    first = plan.n + plan.block_rows
    return partner_ref[first : first + 16, :][0:1, :].astype(F32)


def pair_tiles(plan, near_row, local, pay, partner, acc):
    def kernel(near_ref, local_ref, pay_ref, partner_ref, acc_in, mine_ref, theirs_ref, form_ref):
        place = lax.axis_index("leaf")
        core = lax.rem(place, 2)
        mine_ref[...] = acc_in[...]
        theirs_ref[...] = jnp.zeros_like(theirs_ref)
        row = flags_of(plan, partner_ref)

        @pl.when(listed(near_ref, place + 1 - 2 * core))
        def _():
            source = partner_ref.at[pl.ds(plan.n, plan.block_rows), :]
            add_half(plan, mine_ref, local_ref, slice(0, plan.n), source, form_ref, True)

        @pl.when(pick(row, place) > 0)
        def _():
            add_half(plan, theirs_ref, partner_ref, slice(0, plan.n), pay_ref.at[core], form_ref, True)

    shape = jax.ShapeDtypeStruct((plan.n, plan.rhs), F32)
    return call(
        kernel,
        [shape, shape],
        [(near_row, SMEM), (local, VMEM), (pay, VMEM), (partner, VMEM), (acc, VMEM)],
        scratch=[VMEM((LANES, plan.half), BF16)],
        flops=2 * plan.n * plan.n * 512,
        name="pair_tiles",
    )


def side_tiles(plan, near_row, local, partner, full, passed, mine, theirs, reach):
    def kernel(near_ref, local_ref, partner_ref, full_ref, passed_ref, mine_in, theirs_in, mine_ref, theirs_ref, form_ref):
        place = lax.axis_index("leaf")
        core = lax.rem(place, 2)
        away = 2 * core - 1
        mine_ref[...] = mine_in[...]
        theirs_ref[...] = theirs_in[...]
        row = flags_of(plan, partner_ref)
        first = place + away * reach
        second = place - away - away * reach
        for source, at in ((full_ref.at[core], first), (passed_ref, second)):
            on_mine = listed(near_ref, at)
            on_theirs = pick(row, at) > 0

            @pl.when(on_mine)
            def _():
                add_half(plan, mine_ref, local_ref, slice(0, plan.n), source, form_ref, True)

            @pl.when(on_theirs)
            def _():
                add_half(plan, theirs_ref, partner_ref, slice(0, plan.n), source, form_ref, True)

    shape = jax.ShapeDtypeStruct((plan.n, plan.rhs), F32)
    return call(
        kernel,
        [shape, shape],
        [(near_row, SMEM), (local, VMEM), (partner, VMEM), (full, VMEM), (passed, VMEM), (mine, VMEM), (theirs, VMEM)],
        scratch=[VMEM((LANES, plan.half), BF16)],
        flops=2 * 2 * plan.n * plan.n * 512,
        name="side_tiles",
    )


def last_tile(plan, near_row, local, far_pay, mine, returned, iterate, wanted, step_size, basis, local_coef):
    def kernel(near_ref, local_ref, pay_ref, mine_ref, returned_ref, iterate_ref, wanted_ref, step_ref, basis_ref, coef_ref, out_ref, form_ref):
        place = lax.axis_index("leaf")
        core = lax.rem(place, 2)
        away = 2 * core - 1
        out_ref[...] = mine_ref[...] + returned_ref[...] + matmul(basis_ref[...], coef_ref[...])

        @pl.when(listed(near_ref, place + 3 * away))
        def _():
            for h in range(2):
                add_half(plan, out_ref, local_ref, slice(0, plan.n), pay_ref.at[h], form_ref, True)

        out_ref[...] = iterate_ref[...] + step_ref[...] * (wanted_ref[...] - out_ref[...])

    return call(
        kernel,
        jax.ShapeDtypeStruct((plan.n, plan.rhs), F32),
        [
            (near_row, SMEM),
            (local, VMEM),
            (far_pay, VMEM),
            (mine, VMEM),
            (returned, VMEM),
            (iterate, VMEM),
            (wanted, VMEM),
            (step_size.reshape(1, -1), VMEM),
            (basis, VMEM),
            (local_coef, VMEM),
        ],
        scratch=[VMEM((LANES, plan.half), BF16)],
        flops=2 * plan.n * plan.n * 512,
        name="last_tile",
    )


def skeleton_rows(rank, dim):
    return (rank // LANES) * dim


def upward(basis, pay, transfer, leaf_skeleton, cluster_skeleton, plan):
    rank, dim = leaf_skeleton.shape[1:]

    def skeleton(ref, out_ref):
        for b in range(rank // LANES):
            out_ref[rank + b * dim : rank + (b + 1) * dim, :] = doubled_transpose(
                ref[0, b * LANES : (b + 1) * LANES, :]
            )

    def kernel(basis_ref, pay_ref, transfer_ref, leaf_ref, cluster_ref, down_ref, up_ref):
        total = jnp.zeros((rank, plan.rhs), F32)
        for h in range(2):
            total = total + contract(
                basis_ref[h * plan.half : (h + 1) * plan.half, :], pay_ref[h, 0 : plan.half, :], ((0,), (0,))
            )
        coef = total.astype(BF16)
        down_ref[0:rank, :] = coef
        skeleton(leaf_ref, down_ref)
        up_ref[0:rank, :] = contract(transfer_ref[0], coef, ((0,), (0,))).astype(BF16)
        skeleton(cluster_ref, up_ref)

    rows = rank + skeleton_rows(rank, dim)
    return call(
        kernel,
        [jax.ShapeDtypeStruct((rows, plan.rhs), BF16)] * 2,
        [(basis, VMEM), (pay, VMEM), (transfer, VMEM), (leaf_skeleton, VMEM), (cluster_skeleton, VMEM)],
        flops=2 * plan.n * rank * plan.rhs,
        name="upward",
    )


def add_far(total, left, block_ref, first, rank, dim):
    right = jnp.concatenate(
        [right_form(block_ref[first + rank + b * dim : first + rank + (b + 1) * dim, :]) for b in range(rank // LANES)],
        axis=1,
    )
    return total + matmul(tile(left, right), block_ref[first : first + rank, :])


def across(cluster_row, cluster_skeleton, own, others, distances):
    rank, dim = cluster_skeleton.shape[1:]
    count = len(others)

    def kernel(far_ref, skeleton_ref, own_ref, *refs):
        out_ref, total_ref = refs[count], refs[count + 1]
        me = lax.axis_index("group")
        left = left_form(skeleton_ref[0])
        total_ref[...] = jnp.zeros_like(total_ref)

        def include(at, block_ref):
            @pl.when(far_ref[0, at] > 0)
            def _():
                total_ref[...] = add_far(total_ref[...], left, block_ref, 0, rank, dim)

        include(me, own_ref)
        for k in range(count):
            include(distances(me, k), refs[k])
        out_ref[...] = total_ref[...].astype(BF16)

    return call(
        kernel,
        jax.ShapeDtypeStruct((rank, LANES), BF16),
        [(cluster_row, SMEM), (cluster_skeleton, VMEM), (own, VMEM)] + [(o, VMEM) for o in others],
        scratch=[VMEM((rank, LANES), F32)],
        flops=2 * 4 * rank * rank * 512,
        name="across",
    )


def down(far_row, leaf_skeleton, transfer, blocks, shares, xors):
    rank, dim = leaf_skeleton.shape[1:]
    rows = rank + skeleton_rows(rank, dim)

    def kernel(far_ref, skeleton_ref, transfer_ref, blocks_ref, share_ref, out_ref, total_ref):
        place = lax.axis_index("leaf")
        left = left_form(skeleton_ref[0])
        lower = share_ref[...]
        total_ref[...] = matmul(transfer_ref[0], lower)
        for k, other in enumerate(xors):

            @pl.when(far_ref[0, place ^ other] > 0)
            def _():
                total_ref[...] = add_far(total_ref[...], left, blocks_ref, k * rows, rank, dim)

        out_ref[...] = total_ref[...].astype(BF16)

    return call(
        kernel,
        jax.ShapeDtypeStruct((rank, LANES), BF16),
        [(far_row, SMEM), (leaf_skeleton, VMEM), (transfer, VMEM), (blocks, VMEM), (shares, VMEM)],
        scratch=[VMEM((rank, LANES), F32)],
        flops=2 * 8 * rank * rank * 512,
        name="down",
    )


def routed(block, axis, target):
    size = lax.axis_size(axis)
    route = [(i, target(i)) for i in range(size) if 0 <= target(i) < size]
    return lax.ppermute(block, axis, route)


def body(
    points,
    ordering,
    iterate,
    target,
    step_size,
    leaf_basis,
    transfer,
    leaf_skeleton,
    cluster_skeleton,
    near_table,
    far_table,
    cluster_far,
):
    plan = Plan(points, iterate)
    leaves = lax.axis_size("leaf")
    groups = lax.axis_size("group")
    core = lax.rem(lax.axis_index("leaf"), 2)

    pay, local = prepare(plan, near_table, iterate, points)
    partner = routed(local, "leaf", lambda i: i ^ 1)
    over = routed(pay, "leaf", lambda i: i + 2 - 4 * (i % 2))
    coef_block, up_block = upward(leaf_basis, pay, transfer, leaf_skeleton, cluster_skeleton, plan)
    others = [routed(up_block, "group", lambda i, k=k: i ^ k) for k in range(1, groups)]
    mine = own_tile(plan, local, pay)
    mine, theirs = pair_tiles(plan, near_table, local, pay, partner, mine)
    share = across(cluster_far, cluster_skeleton, up_block, others, lambda me, k: me ^ (k + 1))

    blocks, shares, xors = coef_block, share, [0]
    bit = leaves // 2
    while bit:
        rows = blocks.shape[0]
        got = routed(jnp.concatenate([blocks, shares], axis=0), "leaf", lambda i, bit=bit: i ^ bit)
        blocks = jnp.concatenate([blocks, got[:rows]], axis=0)
        shares = (shares.astype(F32) + got[rows:].astype(F32)).astype(BF16)
        xors = xors + [x ^ bit for x in xors]
        bit //= 2
    local_coef = down(far_table, leaf_skeleton, transfer, blocks, shares, xors)

    beside = routed(pay, "leaf", lambda i: i - 1 + 2 * (i % 2))
    over_half = routed(lax.dynamic_index_in_dim(over, 1 - core, 0, keepdims=False), "leaf", lambda i: i ^ 1)
    mine, theirs = side_tiles(plan, near_table, local, partner, over, over_half, mine, theirs, 2)
    beside_half = routed(lax.dynamic_index_in_dim(beside, 1 - core, 0, keepdims=False), "leaf", lambda i: i ^ 1)
    third = routed(beside, "leaf", lambda i: i + 2 - 4 * (i % 2))
    mine, theirs = side_tiles(plan, near_table, local, partner, beside, beside_half, mine, theirs, 1)
    returned = routed(theirs, "leaf", lambda i: i ^ 1)
    wanted = target[ordering[0]]
    return last_tile(
        plan, near_table, local, third, mine, returned, iterate, wanted, step_size, leaf_basis, local_coef
    )


def solution(mesh):
    return jax.shard_map(
        body,
        mesh=mesh,
        in_specs=(
            P(("group", "leaf"), None),
            P(("group", "leaf"), None),
            P(("group", "leaf"), None),
            P(("group", "leaf"), None),
            P(),
            P(("group", "leaf"), None),
            P(("group", "leaf"), None, None),
            P(("group", "leaf"), None, None),
            P("group", None, None),
            P(("group", "leaf"), None),
            P(("group", "leaf"), None),
            P("group", None),
        ),
        out_specs=P(("group", "leaf"), None),
        check_vma=False,
    )
```

```python
import math

import jax
import jax.numpy as jnp
from jax import lax
from jax.experimental import pallas as pl
from jax.experimental.pallas import tpu as pltpu
from jax.sharding import PartitionSpec as P

LANES = 128
COLS = 256
ROWS = 1024
FLAG_ROWS = 16
SHIFT = 66.0
LOG2E = math.log2(math.e)
VMEM = pltpu.VMEM
SMEM = pltpu.SMEM
ANY = pl.ANY
F32 = jnp.float32
BF16 = jnp.bfloat16


def contract(left, right, dims):
    return lax.dot_general(left, right, (dims, ((), ())), preferred_element_type=F32)


def matmul(left, right):
    return contract(left, right, ((1,), (0,)))


def call(kernel, outs, ins, scratch=(), flops=0, limit=16, name=None, aliases=None):
    single = not isinstance(outs, (list, tuple))
    shapes = [outs] if single else list(outs)
    with jax.named_scope(name):
        results = pl.pallas_call(
            kernel,
            out_shape=shapes,
            in_specs=[pl.BlockSpec(memory_space=space) for _, space in ins],
            out_specs=[pl.BlockSpec(memory_space=VMEM)] * len(shapes),
            scratch_shapes=list(scratch),
            input_output_aliases=aliases or {},
            compiler_params=pltpu.CompilerParams(vmem_limit_bytes=limit << 20),
            cost_estimate=pl.CostEstimate(
                flops=int(flops), bytes_accessed=sum(a.size * a.dtype.itemsize for a, _ in ins), transcendentals=0
            ),
            name=name,
        )(*[a for a, _ in ins])
    return results[0] if single else results


def shaped(*shape, dtype=BF16):
    return jax.ShapeDtypeStruct(shape, dtype)


class Plan:
    def __init__(self, points, iterate):
        self.n, self.dim = points.shape
        self.rhs = iterate.shape[1]
        self.half = self.n // 2
        self.blocks = self.half // LANES
        self.flags = self.half + self.blocks * self.dim
        self.rows = self.flags + FLAG_ROWS
        self.tile_flops = 2 * self.n * self.n * 512

    def pay(self):
        return shaped(2, self.rows, self.rhs)

    def acc(self):
        return shaped(2, self.n, self.rhs, dtype=F32)

    def left(self):
        return shaped(2, self.n, self.dim)

    def offset_scratch(self):
        return [VMEM((8, self.half), F32)]


def three_parts(value):
    high = value.astype(BF16).astype(F32)
    rest = value - high
    middle = rest.astype(BF16).astype(F32)
    return high, middle, rest - middle


def extended(doubled, left):
    dim, width = doubled.shape
    wide = doubled.astype(F32)
    parts = three_parts(-0.25 * jnp.sum(wide * wide, axis=0, keepdims=True))
    row = lax.broadcasted_iota(jnp.int32, (LANES - dim, width), 0)
    ones, first = (0, 3) if left else (3, 0)
    below = jnp.where((row >= ones) & (row < ones + 3), 1.0, 0.0)
    for k, part in enumerate(parts):
        below = jnp.where(row == first + k, part, below)
    return jnp.concatenate([0.5 * wide if left else wide, below], axis=0)


def small_left(doubled):
    width = doubled.shape[1]
    return jnp.concatenate(
        [extended(doubled[:, k : k + LANES], True).T.astype(BF16) for k in range(0, width, LANES)], axis=0
    )


def doubled_of(ref):
    return (2.0 * ref[0].astype(F32)).astype(BF16)


def left_block(doubled):
    twice = jnp.concatenate([doubled, doubled], axis=0).astype(F32)
    return (0.5 * twice.T)[:, 0 : doubled.shape[0]].astype(BF16)


def doubled_block(plan, ref, b):
    return ref[plan.half + b * plan.dim : plan.half + (b + 1) * plan.dim, :]


def fill_left(plan, out_ref, ref, h):
    for b in range(plan.blocks):
        first = h * plan.half + b * LANES
        out_ref[first : first + LANES, :] = left_block(doubled_block(plan, ref, b))


def norms(doubled):
    wide = doubled.astype(F32)
    return (0.25 * LOG2E) * jnp.sum(wide * wide, axis=0, keepdims=True)


def fill_offset(plan, offset_ref, ref):
    for b in range(plan.blocks):
        offset_ref[0:1, b * LANES : (b + 1) * LANES] = -norms(doubled_block(plan, ref, b)) - SHIFT


def half_tile(plan, acc_ref, left_ref, source_ref, offset_ref):
    for r in range(0, plan.n, ROWS):
        left = left_ref[r : r + ROWS, :]
        total = acc_ref[r : r + ROWS, :]
        for c in range(0, plan.half, COLS):
            cols = slice(c, c + COLS)
            right = jnp.concatenate(
                [doubled_block(plan, source_ref, b) for b in range(c // LANES, (c + COLS) // LANES)], axis=1
            )
            power = matmul(left, right) * LOG2E + offset_ref[0:1, cols]
            total = total + matmul(jnp.exp2(power).astype(BF16), source_ref[cols, :])
        acc_ref[r : r + ROWS, :] = total


def pick(row, place):
    lane = lax.broadcasted_iota(jnp.int32, row.shape, 1)
    return jnp.sum(jnp.where(lane == place, row, 0.0)) > 0


def listed(row_ref, place):
    size = row_ref.shape[1]
    inside = (place >= 0) & (place < size)
    return inside & (row_ref[0, jnp.clip(place, 0, size - 1)] > 0)


def skeleton_rows(rank, dim):
    return (rank // LANES) * dim


def prepare(plan, near_row, iterate, points_t, basis, transfer, leaf_t, cluster_t):
    size = near_row.shape[1]
    n, half, dim = plan.n, plan.half, plan.dim
    rank = basis.shape[1]

    def kernel(near_ref, iterate_hbm, points_hbm, basis_hbm, transfer_ref, leaf_ref, cluster_ref, pay_ref, down_ref, up_ref, iterate_ref, points_ref, basis_ref, sems):
        copies = [
            pltpu.make_async_copy(points_hbm, points_ref, sems.at[0]),
            pltpu.make_async_copy(iterate_hbm, iterate_ref, sems.at[1]),
            pltpu.make_async_copy(basis_hbm, basis_ref, sems.at[2]),
        ]
        for copy in copies:
            copy.start()
        lane = lax.broadcasted_iota(jnp.int32, (FLAG_ROWS, LANES), 1)
        row = jnp.zeros((FLAG_ROWS, LANES), F32)
        for k in range(size):
            row = jnp.where(lane == k, near_ref[0, k].astype(F32), row)

        def skeleton(ref, out_ref):
            doubled = doubled_of(ref)
            for b in range(rank // LANES):
                out_ref[rank + b * dim : rank + (b + 1) * dim, :] = doubled[:, b * LANES : (b + 1) * LANES]

        skeleton(leaf_ref, down_ref)
        skeleton(cluster_ref, up_ref)
        copies[0].wait()
        for h in range(2):
            pay_ref[h, plan.flags :, :] = row.astype(BF16)
            for b in range(plan.blocks):
                first = h * half + b * LANES
                pay_ref[h, half + b * dim : half + (b + 1) * dim, :] = (
                    2.0 * points_ref[:, first : first + LANES].astype(F32)
                ).astype(BF16)
        copies[1].wait()
        for h in range(2):
            pay_ref[h, 0:half, :] = iterate_ref[h * half : (h + 1) * half, :].astype(BF16)
        copies[2].wait()
        total = jnp.zeros((rank, plan.rhs), F32)
        for h in range(2):
            total = total + contract(
                basis_ref[h * half : (h + 1) * half, :], pay_ref[h, 0:half, :], ((0,), (0,))
            )
        coef = total.astype(BF16)
        down_ref[0:rank, :] = coef
        up_ref[0:rank, :] = contract(transfer_ref[0], coef, ((0,), (0,))).astype(BF16)

    rows = rank + skeleton_rows(rank, dim)
    return call(
        kernel,
        [plan.pay(), shaped(rows, plan.rhs), shaped(rows, plan.rhs)],
        [(near_row, SMEM), (iterate, ANY), (points_t, ANY), (basis, ANY), (transfer, VMEM), (leaf_t, VMEM), (cluster_t, VMEM)],
        scratch=[
            VMEM(iterate.shape, F32),
            VMEM(points_t.shape, BF16),
            VMEM(basis.shape, BF16),
            pltpu.SemaphoreType.DMA((3,)),
        ],
        flops=2 * n * rank * plan.rhs,
        name="prepare",
    )


def own_tile(plan, pay):
    def kernel(pay_ref, acc_ref, left_ref, offset_ref):
        acc_ref[...] = jnp.zeros_like(acc_ref)
        for h in range(2):
            fill_left(plan, left_ref, pay_ref.at[h], h)

        @pl.loop(0, 2)
        def _(h):
            fill_offset(plan, offset_ref, pay_ref.at[h])
            half_tile(plan, acc_ref.at[0], left_ref, pay_ref.at[h], offset_ref)

    return call(
        kernel,
        plan.acc(),
        [(pay, VMEM)],
        scratch=[VMEM(plan.left().shape[1:], BF16)] + plan.offset_scratch(),
        flops=plan.tile_flops,
        name="own_tile",
    )


def pair_tiles(plan, near_row, pay, partner, acc):
    def kernel(near_ref, pay_ref, partner_ref, acc_in, acc_ref, left_ref, row_ref, offset_ref):
        place = lax.axis_index("leaf")
        core = lax.rem(place, 2)
        for h in range(2):
            fill_left(plan, left_ref.at[0], pay_ref.at[h], h)
            fill_left(plan, left_ref.at[1], partner_ref.at[h], h)
        row = partner_ref[0, plan.flags :, :].astype(F32)
        row_ref[...] = row

        @pl.when(listed(near_ref, place + 1 - 2 * core))
        def _():
            fill_offset(plan, offset_ref, partner_ref.at[core])
            half_tile(plan, acc_ref.at[0], left_ref.at[0], partner_ref.at[core], offset_ref)

        @pl.when(pick(row, place))
        def _():
            fill_offset(plan, offset_ref, pay_ref.at[core])
            half_tile(plan, acc_ref.at[1], left_ref.at[1], pay_ref.at[core], offset_ref)

    return call(
        kernel,
        [plan.acc(), plan.left(), shaped(FLAG_ROWS, LANES, dtype=F32)],
        [(near_row, SMEM), (pay, VMEM), (partner, VMEM), (acc, VMEM)],
        scratch=plan.offset_scratch(),
        flops=plan.tile_flops,
        name="pair_tiles",
        aliases={3: 0},
    )


def side_tiles(plan, near_row, row, left, full, passed, acc, reach, last):
    def kernel(near_ref, row_in, left_ref, full_ref, passed_ref, acc_in, acc_ref, *refs):
        offset_ref = refs[-1]
        place = lax.axis_index("leaf")
        core = lax.rem(place, 2)
        away = 2 * core - 1
        row = row_in[...]
        first = place + away * reach
        second = place - away - away * reach
        for source, at in ((full_ref.at[core], first), (passed_ref.at[core], second)):
            on_mine = listed(near_ref, at)
            on_theirs = pick(row, at)

            @pl.when(on_mine | on_theirs)
            def _():
                fill_offset(plan, offset_ref, source)

            @pl.loop(0, 2)
            def _(t):
                @pl.when(jnp.where(t == 0, on_mine, on_theirs))
                def _():
                    half_tile(plan, acc_ref.at[t], left_ref.at[t], source, offset_ref)

        if last:
            refs[0][...] = acc_ref[1]

    outs = [plan.acc()] + ([shaped(plan.n, plan.rhs, dtype=F32)] if last else [])
    return call(
        kernel,
        outs,
        [(near_row, SMEM), (row, VMEM), (left, VMEM), (full, VMEM), (passed, VMEM), (acc, VMEM)],
        scratch=plan.offset_scratch(),
        flops=2 * plan.tile_flops,
        name="side_tiles_b" if last else "side_tiles_a",
        aliases={5: 0},
    )


def wanted_rows(ordering, target):
    n, rhs = target.shape
    step = 2 * LANES

    def kernel(order_ref, target_hbm, out_ref, target_ref, halves_ref, sem):
        copy = pltpu.make_async_copy(target_hbm, target_ref, sem)
        copy.start()
        copy.wait()
        value = target_ref[...]
        high = value.astype(BF16)
        halves_ref[:, 0:rhs] = high
        halves_ref[:, rhs:] = (value - high.astype(F32)).astype(BF16)
        lane = lax.broadcasted_iota(jnp.int32, (LANES, LANES), 1).astype(F32)

        @pl.loop(0, n // step)
        def _(i):
            picks = []
            for k in range(step // LANES):
                rows = pl.ds(pl.multiple_of(i * step + k * LANES, LANES), LANES)
                index = jnp.broadcast_to(order_ref[:, rows].astype(F32), (LANES, LANES)).T
                picks.append(
                    jnp.concatenate(
                        [jnp.where(index == lane + c, 1.0, 0.0).astype(BF16) for c in range(0, n, LANES)], axis=1
                    )
                )
            both = matmul(jnp.concatenate(picks, axis=0), halves_ref[...])
            out_ref[pl.ds(pl.multiple_of(i * step, step), step), :] = both[:, 0:rhs] + both[:, rhs:]

    return call(
        kernel,
        shaped(n, rhs, dtype=F32),
        [(ordering, VMEM), (target, ANY)],
        scratch=[VMEM((n, rhs), F32), VMEM((n, 2 * rhs), BF16), pltpu.SemaphoreType.DMA],
        flops=n * n * 512,
        name="wanted_rows",
    )


def last_tile(plan, near_row, pay, left, third, acc, returned, iterate, wanted, step_size, basis, local):
    def kernel(near_ref, pay_ref, left_ref, third_ref, acc_ref, returned_ref, iterate_ref, wanted_ref, step_ref, basis_ref, local_ref, out_ref, offset_ref):
        place = lax.axis_index("leaf")
        away = 2 * lax.rem(place, 2) - 1
        out_ref[...] = acc_ref[0] + returned_ref[...]

        @pl.when(listed(near_ref, place + 3 * away))
        def _():
            @pl.loop(0, 2)
            def _(h):
                fill_offset(plan, offset_ref, third_ref.at[h])
                half_tile(plan, out_ref, left_ref.at[0], third_ref.at[h], offset_ref)

        for h in range(2):
            for b in range(plan.blocks):
                first = h * plan.half + b * LANES
                rows = slice(first, first + LANES)
                power = SHIFT - norms(doubled_block(plan, pay_ref.at[h], b))
                factor = jnp.exp2(jnp.broadcast_to(power, (LANES, LANES)).T)
                image = matmul(basis_ref[rows, :], local_ref[...]) + factor * out_ref[rows, :]
                out_ref[rows, :] = iterate_ref[rows, :] + step_ref[...] * (wanted_ref[rows, :] - image)

    return call(
        kernel,
        shaped(plan.n, plan.rhs, dtype=F32),
        [
            (near_row, SMEM),
            (pay, VMEM),
            (left, VMEM),
            (third, VMEM),
            (acc, VMEM),
            (returned, VMEM),
            (iterate, VMEM),
            (wanted, VMEM),
            (step_size.reshape(1, -1), VMEM),
            (basis, VMEM),
            (local, VMEM),
        ],
        scratch=plan.offset_scratch(),
        flops=plan.tile_flops,
        name="last_tile",
    )


def add_far(total, left, block_ref, first, rank, dim):
    right = jnp.concatenate(
        [
            extended(block_ref[first + rank + b * dim : first + rank + (b + 1) * dim, :], False).astype(BF16)
            for b in range(rank // LANES)
        ],
        axis=1,
    )
    return total + matmul(jnp.exp(matmul(left, right)).astype(BF16), block_ref[first : first + rank, :])


def across(cluster_row, cluster_t, own, others, distances, down_block):
    dim, rank = cluster_t.shape[1:]
    count = len(others)
    rows = down_block.shape[0]

    def kernel(far_ref, skeleton_ref, down_ref, own_ref, *refs):
        out_ref, total_ref = refs[count], refs[count + 1]
        me = lax.axis_index("group")
        left = small_left(doubled_of(skeleton_ref))
        total_ref[...] = jnp.zeros_like(total_ref)
        out_ref[0:rows, :] = down_ref[...]

        def include(at, block_ref):
            @pl.when(far_ref[0, at] > 0)
            def _():
                total_ref[...] = add_far(total_ref[...], left, block_ref, 0, rank, dim)

        include(me, own_ref)
        for k in range(count):
            include(distances(me, k), refs[k])
        out_ref[rows:, :] = total_ref[...].astype(BF16)

    return call(
        kernel,
        shaped(rows + rank, LANES),
        [(cluster_row, SMEM), (cluster_t, VMEM), (down_block, VMEM), (own, VMEM)] + [(o, VMEM) for o in others],
        scratch=[VMEM((rank, LANES), F32)],
        flops=2 * 4 * rank * rank * 512,
        name="across",
    )


def joined(mine, got, rank, name):
    rows = mine.shape[0] - rank

    def kernel(mine_ref, got_ref, out_ref):
        out_ref[0:rows, :] = mine_ref[0:rows, :]
        out_ref[rows : 2 * rows, :] = got_ref[0:rows, :]
        out_ref[2 * rows :, :] = (mine_ref[rows:, :].astype(F32) + got_ref[rows:, :].astype(F32)).astype(BF16)

    return call(kernel, shaped(2 * rows + rank, LANES), [(mine, VMEM), (got, VMEM)], name=name)


def down(far_row, leaf_t, transfer, mine, got, xors):
    dim, rank = leaf_t.shape[1:]
    rows = rank + skeleton_rows(rank, dim)
    count = (mine.shape[0] - rank) // rows

    def kernel(far_ref, skeleton_ref, transfer_ref, mine_ref, got_ref, out_ref, total_ref):
        place = lax.axis_index("leaf")
        left = small_left(doubled_of(skeleton_ref))
        lower = (mine_ref[count * rows :, :].astype(F32) + got_ref[count * rows :, :].astype(F32)).astype(BF16)
        total_ref[...] = matmul(transfer_ref[0], lower)
        for k, other in enumerate(xors):
            block_ref, at = (mine_ref, k) if k < count else (got_ref, k - count)

            @pl.when(far_ref[0, place ^ other] > 0)
            def _():
                total_ref[...] = add_far(total_ref[...], left, block_ref, at * rows, rank, dim)

        out_ref[...] = total_ref[...].astype(BF16)

    return call(
        kernel,
        shaped(rank, LANES),
        [(far_row, SMEM), (leaf_t, VMEM), (transfer, VMEM), (mine, VMEM), (got, VMEM)],
        scratch=[VMEM((rank, LANES), F32)],
        flops=2 * 8 * rank * rank * 512,
        name="down",
    )


def routed(block, axis, target, name):
    size = lax.axis_size(axis)
    route = [(i, target(i)) for i in range(size) if 0 <= target(i) < size]
    with jax.named_scope(name):
        return lax.ppermute(block, axis, route)


def over_chips(i):
    return i + 2 - 4 * (i % 2)


def beside_chips(i):
    return i - 1 + 2 * (i % 2)


def on_chip(i):
    return i ^ 1


def body(
    points,
    ordering,
    iterate,
    target,
    step_size,
    leaf_basis,
    transfer,
    leaf_skeleton,
    cluster_skeleton,
    near_table,
    far_table,
    cluster_far,
):
    plan = Plan(points, iterate)
    leaves = lax.axis_size("leaf")
    groups = lax.axis_size("group")
    rank = leaf_basis.shape[1]
    leaf_t = jnp.swapaxes(leaf_skeleton, 1, 2)
    cluster_t = jnp.swapaxes(cluster_skeleton, 1, 2)

    pay, down_block, up_block = prepare(
        plan, near_table, iterate, points.T, leaf_basis, transfer, leaf_t, cluster_t
    )
    partner = routed(pay, "leaf", on_chip, "swap")
    over = routed(pay, "leaf", over_chips, "over")
    others = [routed(up_block, "group", lambda i, k=k: i ^ k, f"group{k}") for k in range(1, groups)]
    acc = own_tile(plan, pay)
    mine = across(cluster_far, cluster_t, up_block, others, lambda me, k: me ^ (k + 1), down_block)
    acc, left, row = pair_tiles(plan, near_table, pay, partner, acc)

    xors, bit = [0], leaves // 2
    while True:
        got = routed(mine, "leaf", lambda i, bit=bit: i ^ bit, f"far{bit}")
        xors = xors + [x ^ bit for x in xors]
        if bit == 1:
            break
        mine = joined(mine, got, rank, f"joined{bit}")
        bit //= 2
    local = down(far_table, leaf_t, transfer, mine, got, xors)

    beside = routed(pay, "leaf", beside_chips, "beside")
    over_passed = routed(over, "leaf", on_chip, "over_passed")
    (acc,) = side_tiles(plan, near_table, row, left, over, over_passed, acc, 2, False)
    beside_passed = routed(beside, "leaf", on_chip, "beside_passed")
    third = routed(beside, "leaf", over_chips, "third")
    acc, theirs = side_tiles(plan, near_table, row, left, beside, beside_passed, acc, 1, True)
    returned = routed(theirs, "leaf", on_chip, "returned")
    wanted = wanted_rows(ordering, target)
    return last_tile(
        plan, near_table, pay, left, third, acc, returned, iterate, wanted, step_size, leaf_basis, local
    )


def solution(mesh):
    return jax.shard_map(
        body,
        mesh=mesh,
        in_specs=(
            P(("group", "leaf"), None),
            P(("group", "leaf"), None),
            P(("group", "leaf"), None),
            P(("group", "leaf"), None),
            P(),
            P(("group", "leaf"), None),
            P(("group", "leaf"), None, None),
            P(("group", "leaf"), None, None),
            P("group", None, None),
            P(("group", "leaf"), None),
            P(("group", "leaf"), None),
            P("group", None),
        ),
        out_specs=P(("group", "leaf"), None),
        check_vma=False,
    )
```

```python
import math

import jax
import jax.numpy as jnp
from jax import lax
from jax.experimental import pallas as pl
from jax.experimental.pallas import tpu as pltpu
from jax.sharding import PartitionSpec as P


LANES = 128
COLS = 256
ROWS = 1024
FLAG_ROWS = 16
SHIFT = 66.0
LOG2E = math.log2(math.e)
VMEM = pltpu.VMEM
SMEM = pltpu.SMEM
HBM = pltpu.HBM
F32 = jnp.float32
BF16 = jnp.bfloat16


def contract(left, right, dims):
    return lax.dot_general(left, right, (dims, ((), ())), preferred_element_type=F32)


def matmul(left, right):
    return contract(left, right, ((1,), (0,)))


def call(kernel, outs, ins, scratch=(), flops=0, limit=16, aliases=None):
    single = not isinstance(outs, (list, tuple))
    shapes = [outs] if single else list(outs)
    results = pl.pallas_call(
        kernel,
        out_shape=shapes,
        in_specs=[pl.BlockSpec(memory_space=space) for _, space in ins],
        out_specs=[pl.BlockSpec(memory_space=VMEM)] * len(shapes),
        scratch_shapes=list(scratch),
        input_output_aliases=aliases or {},
        compiler_params=pltpu.CompilerParams(vmem_limit_bytes=limit << 20),
        cost_estimate=pl.CostEstimate(
            flops=int(flops), bytes_accessed=sum(a.size * a.dtype.itemsize for a, _ in ins), transcendentals=0
        ),
    )(*[a for a, _ in ins])
    return results[0] if single else results


def shaped(*shape, dtype=BF16):
    return jax.ShapeDtypeStruct(shape, dtype)


class Plan:
    def __init__(self, points, iterate):
        self.n, self.dim = points.shape
        self.rhs = iterate.shape[1]
        self.half = self.n // 2
        self.blocks = self.half // LANES
        self.flags = self.half + self.blocks * self.dim
        self.rows = self.flags + FLAG_ROWS
        self.tile_flops = 2 * self.n * self.n * 512

    def pay(self):
        return shaped(2, self.rows, self.rhs)

    def acc(self):
        return shaped(2, self.n, self.rhs, dtype=F32)

    def left(self):
        return shaped(2, self.n, self.dim)

    def offset_scratch(self):
        return [VMEM((8, self.half), F32)]


def three_parts(value):
    high = value.astype(BF16).astype(F32)
    rest = value - high
    middle = rest.astype(BF16).astype(F32)
    return high, middle, rest - middle


def extended(doubled, left):
    dim, width = doubled.shape
    wide = doubled.astype(F32)
    parts = three_parts(-0.25 * jnp.sum(wide * wide, axis=0, keepdims=True))
    row = lax.broadcasted_iota(jnp.int32, (LANES - dim, width), 0)
    ones, first = (0, 3) if left else (3, 0)
    below = jnp.where((row >= ones) & (row < ones + 3), 1.0, 0.0)
    for k, part in enumerate(parts):
        below = jnp.where(row == first + k, part, below)
    return jnp.concatenate([0.5 * wide if left else wide, below], axis=0)


def small_left(doubled):
    width = doubled.shape[1]
    return jnp.concatenate(
        [extended(doubled[:, k : k + LANES], True).T.astype(BF16) for k in range(0, width, LANES)], axis=0
    )


def doubled_of(ref):
    return (2.0 * ref[0].astype(F32)).astype(BF16)


def left_block(doubled):
    twice = jnp.concatenate([doubled, doubled], axis=0).astype(F32)
    return (0.5 * twice.T)[:, 0 : doubled.shape[0]].astype(BF16)


def doubled_block(plan, ref, b):
    return ref[plan.half + b * plan.dim : plan.half + (b + 1) * plan.dim, :]


def fill_left(plan, out_ref, ref, h):
    for b in range(plan.blocks):
        first = h * plan.half + b * LANES
        out_ref[first : first + LANES, :] = left_block(doubled_block(plan, ref, b))


def norms(doubled):
    wide = doubled.astype(F32)
    return (0.25 * LOG2E) * jnp.sum(wide * wide, axis=0, keepdims=True)


def fill_offset(plan, offset_ref, ref):
    for b in range(plan.blocks):
        offset_ref[0:1, b * LANES : (b + 1) * LANES] = -norms(doubled_block(plan, ref, b)) - SHIFT


def half_tile(plan, acc_ref, left_ref, source_ref, offset_ref):
    for r in range(0, plan.n, ROWS):
        left = left_ref[r : r + ROWS, :]
        total = acc_ref[r : r + ROWS, :]
        for c in range(0, plan.half, COLS):
            cols = slice(c, c + COLS)
            right = jnp.concatenate(
                [doubled_block(plan, source_ref, b) for b in range(c // LANES, (c + COLS) // LANES)], axis=1
            )
            power = matmul(left, right) * LOG2E + offset_ref[0:1, cols]
            total = total + matmul(jnp.exp2(power).astype(BF16), source_ref[cols, :])
        acc_ref[r : r + ROWS, :] = total


def pick(row, place):
    lane = lax.broadcasted_iota(jnp.int32, row.shape, 1)
    return jnp.sum(jnp.where(lane == place, row, 0.0)) > 0


def listed(row_ref, place):
    size = row_ref.shape[1]
    inside = (place >= 0) & (place < size)
    return inside & (row_ref[0, jnp.clip(place, 0, size - 1)] > 0)


def skeleton_rows(rank, dim):
    return (rank // LANES) * dim


def prepare(plan, near_row, iterate, points_t, basis, transfer, leaf_t, cluster_t):
    size = near_row.shape[1]
    n, half, dim = plan.n, plan.half, plan.dim
    rank = basis.shape[1]

    inputs = [points_t, iterate, near_row, leaf_t, cluster_t, basis, transfer]

    def kernel(*refs):
        count = len(inputs)
        sources, (pay_ref, down_ref, up_ref) = refs[:count], refs[count : count + 3]
        points_ref, iterate_ref, near_ref, leaf_ref, cluster_ref, basis_ref, transfer_ref, sems = refs[count + 3 :]
        copies = [
            pltpu.make_async_copy(source, into, sems.at[k])
            for k, (source, into) in enumerate(zip(sources, refs[count + 3 : -1]))
        ]
        for copy in copies:
            copy.start()
        copies[0].wait()
        for h in range(2):
            for b in range(plan.blocks):
                first = h * half + b * LANES
                pay_ref[h, half + b * dim : half + (b + 1) * dim, :] = (
                    2.0 * points_ref[:, first : first + LANES].astype(F32)
                ).astype(BF16)
        copies[1].wait()
        for h in range(2):
            pay_ref[h, 0:half, :] = iterate_ref[h * half : (h + 1) * half, :].astype(BF16)
        for copy in copies[2:]:
            copy.wait()
        lane = lax.broadcasted_iota(jnp.int32, (FLAG_ROWS, LANES), 1)
        row = jnp.zeros((FLAG_ROWS, LANES), F32)
        for k in range(size):
            row = jnp.where(lane == k, near_ref[0, k].astype(F32), row)
        for h in range(2):
            pay_ref[h, plan.flags :, :] = row.astype(BF16)

        def skeleton(ref, out_ref):
            doubled = doubled_of(ref)
            for b in range(rank // LANES):
                out_ref[rank + b * dim : rank + (b + 1) * dim, :] = doubled[:, b * LANES : (b + 1) * LANES]

        skeleton(leaf_ref, down_ref)
        skeleton(cluster_ref, up_ref)
        total = jnp.zeros((rank, plan.rhs), F32)
        for h in range(2):
            total = total + contract(
                basis_ref[h * half : (h + 1) * half, :], pay_ref[h, 0:half, :], ((0,), (0,))
            )
        coef = total.astype(BF16)
        down_ref[0:rank, :] = coef
        up_ref[0:rank, :] = contract(transfer_ref[0], coef, ((0,), (0,))).astype(BF16)

    rows = rank + skeleton_rows(rank, dim)
    return call(
        kernel,
        [plan.pay(), shaped(rows, plan.rhs), shaped(rows, plan.rhs)],
        [(value, HBM) for value in inputs],
        scratch=[(SMEM if value is near_row else VMEM)(value.shape, value.dtype) for value in inputs]
        + [pltpu.SemaphoreType.DMA((len(inputs),))],
        flops=2 * n * rank * plan.rhs,
    )


def own_tile(plan, pay):
    def kernel(pay_ref, acc_ref, left_ref, offset_ref):
        acc_ref[...] = jnp.zeros_like(acc_ref)
        for h in range(2):
            fill_left(plan, left_ref, pay_ref.at[h], h)

        @pl.loop(0, 2)
        def _(h):
            fill_offset(plan, offset_ref, pay_ref.at[h])
            half_tile(plan, acc_ref.at[0], left_ref, pay_ref.at[h], offset_ref)

    return call(
        kernel,
        plan.acc(),
        [(pay, VMEM)],
        scratch=[VMEM(plan.left().shape[1:], BF16)] + plan.offset_scratch(),
        flops=plan.tile_flops,
    )


def pair_tiles(plan, near_row, pay, partner, acc):
    def kernel(near_ref, pay_ref, partner_ref, acc_in, acc_ref, left_ref, row_ref, offset_ref):
        place = lax.axis_index("leaf")
        core = lax.rem(place, 2)
        for h in range(2):
            fill_left(plan, left_ref.at[0], pay_ref.at[h], h)
            fill_left(plan, left_ref.at[1], partner_ref.at[h], h)
        row = partner_ref[0, plan.flags :, :].astype(F32)
        row_ref[...] = row

        @pl.when(listed(near_ref, place + 1 - 2 * core))
        def _():
            fill_offset(plan, offset_ref, partner_ref.at[core])
            half_tile(plan, acc_ref.at[0], left_ref.at[0], partner_ref.at[core], offset_ref)

        @pl.when(pick(row, place))
        def _():
            fill_offset(plan, offset_ref, pay_ref.at[core])
            half_tile(plan, acc_ref.at[1], left_ref.at[1], pay_ref.at[core], offset_ref)

    return call(
        kernel,
        [plan.acc(), plan.left(), shaped(FLAG_ROWS, LANES, dtype=F32)],
        [(near_row, SMEM), (pay, VMEM), (partner, VMEM), (acc, VMEM)],
        scratch=plan.offset_scratch(),
        flops=plan.tile_flops,
        aliases={3: 0},
    )


def side_tiles(plan, near_row, row, left, full, passed, acc, reach, last):
    def kernel(near_ref, row_in, left_ref, full_ref, passed_ref, acc_in, acc_ref, *refs):
        offset_ref = refs[-1]
        place = lax.axis_index("leaf")
        core = lax.rem(place, 2)
        away = 2 * core - 1
        row = row_in[...]
        first = place + away * reach
        second = place - away - away * reach
        for source, at in ((full_ref.at[core], first), (passed_ref.at[core], second)):
            on_mine = listed(near_ref, at)
            on_theirs = pick(row, at)

            @pl.when(on_mine | on_theirs)
            def _():
                fill_offset(plan, offset_ref, source)

            @pl.loop(0, 2)
            def _(t):
                @pl.when(jnp.where(t == 0, on_mine, on_theirs))
                def _():
                    half_tile(plan, acc_ref.at[t], left_ref.at[t], source, offset_ref)

        if last:
            refs[0][...] = acc_ref[1]

    outs = [plan.acc()] + ([shaped(plan.n, plan.rhs, dtype=F32)] if last else [])
    return call(
        kernel,
        outs,
        [(near_row, SMEM), (row, VMEM), (left, VMEM), (full, VMEM), (passed, VMEM), (acc, VMEM)],
        scratch=plan.offset_scratch(),
        flops=2 * plan.tile_flops,
        aliases={5: 0},
    )


def wanted_rows(ordering, target):
    n, rhs = target.shape
    step = 2 * LANES

    def kernel(order_ref, target_hbm, out_ref, target_ref, halves_ref, sem):
        copy = pltpu.make_async_copy(target_hbm, target_ref, sem)
        copy.start()
        copy.wait()
        value = target_ref[...]
        high = value.astype(BF16)
        halves_ref[:, 0:rhs] = high
        halves_ref[:, rhs:] = (value - high.astype(F32)).astype(BF16)
        lane = lax.broadcasted_iota(jnp.int32, (LANES, LANES), 1).astype(F32)

        @pl.loop(0, n // step)
        def _(i):
            picks = []
            for k in range(step // LANES):
                rows = pl.ds(pl.multiple_of(i * step + k * LANES, LANES), LANES)
                index = jnp.broadcast_to(order_ref[:, rows].astype(F32), (LANES, LANES)).T
                picks.append(
                    jnp.concatenate(
                        [jnp.where(index == lane + c, 1.0, 0.0).astype(BF16) for c in range(0, n, LANES)], axis=1
                    )
                )
            both = matmul(jnp.concatenate(picks, axis=0), halves_ref[...])
            out_ref[pl.ds(pl.multiple_of(i * step, step), step), :] = both[:, 0:rhs] + both[:, rhs:]

    return call(
        kernel,
        shaped(n, rhs, dtype=F32),
        [(ordering, VMEM), (target, HBM)],
        scratch=[VMEM((n, rhs), F32), VMEM((n, 2 * rhs), BF16), pltpu.SemaphoreType.DMA],
        flops=n * n * 512,
    )


def last_tile(plan, near_row, pay, left, third, acc, returned, iterate, wanted, step_size, basis, local):
    def kernel(near_ref, pay_ref, left_ref, third_ref, acc_ref, returned_ref, iterate_ref, wanted_ref, step_ref, basis_ref, local_ref, out_ref, offset_ref):
        place = lax.axis_index("leaf")
        away = 2 * lax.rem(place, 2) - 1
        out_ref[...] = acc_ref[0] + returned_ref[...]

        @pl.when(listed(near_ref, place + 3 * away))
        def _():
            @pl.loop(0, 2)
            def _(h):
                fill_offset(plan, offset_ref, third_ref.at[h])
                half_tile(plan, out_ref, left_ref.at[0], third_ref.at[h], offset_ref)

        for h in range(2):
            for b in range(plan.blocks):
                first = h * plan.half + b * LANES
                rows = slice(first, first + LANES)
                power = SHIFT - norms(doubled_block(plan, pay_ref.at[h], b))
                factor = jnp.exp2(jnp.broadcast_to(power, (LANES, LANES)).T)
                image = matmul(basis_ref[rows, :], local_ref[...]) + factor * out_ref[rows, :]
                out_ref[rows, :] = iterate_ref[rows, :] + step_ref[...] * (wanted_ref[rows, :] - image)

    return call(
        kernel,
        shaped(plan.n, plan.rhs, dtype=F32),
        [
            (near_row, SMEM),
            (pay, VMEM),
            (left, VMEM),
            (third, VMEM),
            (acc, VMEM),
            (returned, VMEM),
            (iterate, VMEM),
            (wanted, VMEM),
            (step_size.reshape(1, -1), VMEM),
            (basis, VMEM),
            (local, VMEM),
        ],
        scratch=plan.offset_scratch(),
        flops=plan.tile_flops,
    )


def add_far(total, left, block_ref, first, rank, dim):
    right = jnp.concatenate(
        [
            extended(block_ref[first + rank + b * dim : first + rank + (b + 1) * dim, :], False).astype(BF16)
            for b in range(rank // LANES)
        ],
        axis=1,
    )
    return total + matmul(jnp.exp(matmul(left, right)).astype(BF16), block_ref[first : first + rank, :])


def across(cluster_row, cluster_t, own, others, distances, down_block):
    dim, rank = cluster_t.shape[1:]
    count = len(others)
    rows = down_block.shape[0]

    def kernel(far_ref, skeleton_ref, down_ref, own_ref, *refs):
        out_ref, total_ref = refs[count], refs[count + 1]
        me = lax.axis_index("group")
        left = small_left(doubled_of(skeleton_ref))
        total_ref[...] = jnp.zeros_like(total_ref)
        out_ref[0:rows, :] = down_ref[...]

        def include(at, block_ref):
            @pl.when(far_ref[0, at] > 0)
            def _():
                total_ref[...] = add_far(total_ref[...], left, block_ref, 0, rank, dim)

        include(me, own_ref)
        for k in range(count):
            include(distances(me, k), refs[k])
        out_ref[rows:, :] = total_ref[...].astype(BF16)

    return call(
        kernel,
        shaped(rows + rank, LANES),
        [(cluster_row, SMEM), (cluster_t, VMEM), (down_block, VMEM), (own, VMEM)] + [(o, VMEM) for o in others],
        scratch=[VMEM((rank, LANES), F32)],
        flops=2 * 4 * rank * rank * 512,
    )


def joined(mine, got, rank):
    rows = mine.shape[0] - rank

    def kernel(mine_ref, got_ref, out_ref):
        out_ref[0:rows, :] = mine_ref[0:rows, :]
        out_ref[rows : 2 * rows, :] = got_ref[0:rows, :]
        out_ref[2 * rows :, :] = (mine_ref[rows:, :].astype(F32) + got_ref[rows:, :].astype(F32)).astype(BF16)

    return call(kernel, shaped(2 * rows + rank, LANES), [(mine, VMEM), (got, VMEM)])


def down(far_row, leaf_t, transfer, mine, got, xors):
    dim, rank = leaf_t.shape[1:]
    rows = rank + skeleton_rows(rank, dim)
    count = (mine.shape[0] - rank) // rows

    def kernel(far_ref, skeleton_ref, transfer_ref, mine_ref, got_ref, out_ref, total_ref):
        place = lax.axis_index("leaf")
        left = small_left(doubled_of(skeleton_ref))
        lower = (mine_ref[count * rows :, :].astype(F32) + got_ref[count * rows :, :].astype(F32)).astype(BF16)
        total_ref[...] = matmul(transfer_ref[0], lower)
        for k, other in enumerate(xors):
            block_ref, at = (mine_ref, k) if k < count else (got_ref, k - count)

            @pl.when(far_ref[0, place ^ other] > 0)
            def _():
                total_ref[...] = add_far(total_ref[...], left, block_ref, at * rows, rank, dim)

        out_ref[...] = total_ref[...].astype(BF16)

    return call(
        kernel,
        shaped(rank, LANES),
        [(far_row, SMEM), (leaf_t, VMEM), (transfer, VMEM), (mine, VMEM), (got, VMEM)],
        scratch=[VMEM((rank, LANES), F32)],
        flops=2 * 8 * rank * rank * 512,
    )


def routed(block, axis, target):
    size = lax.axis_size(axis)
    route = [(i, target(i)) for i in range(size) if 0 <= target(i) < size]
    return lax.ppermute(block, axis, route)


def over_chips(i):
    return i + 2 - 4 * (i % 2)


def beside_chips(i):
    return i - 1 + 2 * (i % 2)


def on_chip(i):
    return i ^ 1


def body(
    points,
    ordering,
    iterate,
    target,
    step_size,
    leaf_basis,
    transfer,
    leaf_skeleton,
    cluster_skeleton,
    near_table,
    far_table,
    cluster_far,
):
    plan = Plan(points, iterate)
    leaves = lax.axis_size("leaf")
    groups = lax.axis_size("group")
    rank = leaf_basis.shape[1]
    leaf_t = jnp.swapaxes(leaf_skeleton, 1, 2)
    cluster_t = jnp.swapaxes(cluster_skeleton, 1, 2)

    pay, down_block, up_block = prepare(
        plan, near_table, iterate, points.T, leaf_basis, transfer, leaf_t, cluster_t
    )
    partner = routed(pay, "leaf", on_chip)
    over = routed(pay, "leaf", over_chips)
    others = [routed(up_block, "group", lambda i, k=k: i ^ k) for k in range(1, groups)]
    acc = own_tile(plan, pay)
    mine = across(cluster_far, cluster_t, up_block, others, lambda me, k: me ^ (k + 1), down_block)
    acc, left, row = pair_tiles(plan, near_table, pay, partner, acc)

    xors, bit = [0], leaves // 2
    while True:
        got = routed(mine, "leaf", lambda i, bit=bit: i ^ bit)
        xors = xors + [x ^ bit for x in xors]
        if bit == 1:
            break
        mine = joined(mine, got, rank)
        bit //= 2
    local = down(far_table, leaf_t, transfer, mine, got, xors)

    beside = routed(pay, "leaf", beside_chips)
    over_passed = routed(over, "leaf", on_chip)
    (acc,) = side_tiles(plan, near_table, row, left, over, over_passed, acc, 2, False)
    beside_passed = routed(beside, "leaf", on_chip)
    third = routed(beside, "leaf", over_chips)
    acc, theirs = side_tiles(plan, near_table, row, left, beside, beside_passed, acc, 1, True)
    returned = routed(theirs, "leaf", on_chip)
    wanted = wanted_rows(ordering, target)
    return last_tile(
        plan, near_table, pay, left, third, acc, returned, iterate, wanted, step_size, leaf_basis, local
    )


def solution(mesh):
    return jax.shard_map(
        body,
        mesh=mesh,
        in_specs=(
            P(("group", "leaf"), None),
            P(("group", "leaf"), None),
            P(("group", "leaf"), None),
            P(("group", "leaf"), None),
            P(),
            P(("group", "leaf"), None),
            P(("group", "leaf"), None, None),
            P(("group", "leaf"), None, None),
            P("group", None, None),
            P(("group", "leaf"), None),
            P(("group", "leaf"), None),
            P("group", None),
        ),
        out_specs=P(("group", "leaf"), None),
        check_vma=False,
    )
```

```python
import math

import jax
import jax.numpy as jnp
from jax import lax
from jax.experimental import pallas as pl
from jax.experimental.pallas import tpu as pltpu
from jax.sharding import PartitionSpec as P


LANES = 128
COLS = 256
ROWS = 1024
FLAG_ROWS = 16
SHIFT = 66.0
LOG2E = math.log2(math.e)
VMEM = pltpu.VMEM
SMEM = pltpu.SMEM
HBM = pltpu.HBM
F32 = jnp.float32
BF16 = jnp.bfloat16


def contract(left, right, dims):
    return lax.dot_general(left, right, (dims, ((), ())), preferred_element_type=F32)


def matmul(left, right):
    return contract(left, right, ((1,), (0,)))


def call(kernel, outs, ins, scratch=(), flops=0, limit=16, aliases=None, into=VMEM):
    single = not isinstance(outs, (list, tuple))
    shapes = [outs] if single else list(outs)
    results = pl.pallas_call(
        kernel,
        out_shape=shapes,
        in_specs=[pl.BlockSpec(memory_space=space) for _, space in ins],
        out_specs=[pl.BlockSpec(memory_space=into)] * len(shapes),
        scratch_shapes=list(scratch),
        input_output_aliases=aliases or {},
        compiler_params=pltpu.CompilerParams(vmem_limit_bytes=limit << 20),
        cost_estimate=pl.CostEstimate(
            flops=int(flops), bytes_accessed=sum(a.size * a.dtype.itemsize for a, _ in ins), transcendentals=0
        ),
    )(*[a for a, _ in ins])
    return results[0] if single else results


def shaped(*shape, dtype=BF16):
    return jax.ShapeDtypeStruct(shape, dtype)


class Plan:
    def __init__(self, points, iterate):
        self.n, self.dim = points.shape
        self.rhs = iterate.shape[1]
        self.half = self.n // 2
        self.blocks = self.half // LANES
        self.flags = self.half + self.blocks * self.dim
        self.rows = self.flags + FLAG_ROWS
        self.tile_flops = 2 * self.n * self.n * 512

    def pay(self):
        return shaped(2, self.rows, self.rhs)

    def acc(self):
        return shaped(2, self.n, self.rhs, dtype=F32)

    def left(self):
        return shaped(2, self.n, self.dim)

    def offset_scratch(self):
        return [VMEM((8, self.half), F32)]


def three_parts(value):
    high = value.astype(BF16).astype(F32)
    rest = value - high
    middle = rest.astype(BF16).astype(F32)
    return high, middle, rest - middle


def extended(doubled, left):
    dim, width = doubled.shape
    wide = doubled.astype(F32)
    parts = three_parts(-0.25 * jnp.sum(wide * wide, axis=0, keepdims=True))
    row = lax.broadcasted_iota(jnp.int32, (LANES - dim, width), 0)
    ones, first = (0, 3) if left else (3, 0)
    below = jnp.where((row >= ones) & (row < ones + 3), 1.0, 0.0)
    for k, part in enumerate(parts):
        below = jnp.where(row == first + k, part, below)
    return jnp.concatenate([0.5 * wide if left else wide, below], axis=0)


def small_left(doubled):
    width = doubled.shape[1]
    return jnp.concatenate(
        [extended(doubled[:, k : k + LANES], True).T.astype(BF16) for k in range(0, width, LANES)], axis=0
    )


def doubled_of(ref):
    return (2.0 * ref[0].astype(F32)).astype(BF16)


def left_block(doubled):
    twice = jnp.concatenate([doubled, doubled], axis=0).astype(F32)
    return (0.5 * twice.T)[:, 0 : doubled.shape[0]].astype(BF16)


def doubled_block(plan, ref, b):
    return ref[plan.half + b * plan.dim : plan.half + (b + 1) * plan.dim, :]


def fill_left(plan, out_ref, ref, h):
    for b in range(plan.blocks):
        first = h * plan.half + b * LANES
        out_ref[first : first + LANES, :] = left_block(doubled_block(plan, ref, b))


def norms(doubled):
    wide = doubled.astype(F32)
    return (0.25 * LOG2E) * jnp.sum(wide * wide, axis=0, keepdims=True)


def fill_offset(plan, offset_ref, ref):
    for b in range(plan.blocks):
        offset_ref[0:1, b * LANES : (b + 1) * LANES] = -norms(doubled_block(plan, ref, b)) - SHIFT


def half_tile(plan, acc_ref, left_ref, source_ref, offset_ref):
    for r in range(0, plan.n, ROWS):
        left = left_ref[r : r + ROWS, :]
        total = acc_ref[r : r + ROWS, :]
        for c in range(0, plan.half, COLS):
            cols = slice(c, c + COLS)
            right = jnp.concatenate(
                [doubled_block(plan, source_ref, b) for b in range(c // LANES, (c + COLS) // LANES)], axis=1
            )
            power = matmul(left, right) * LOG2E + offset_ref[0:1, cols]
            total = total + matmul(jnp.exp2(power).astype(BF16), source_ref[cols, :])
        acc_ref[r : r + ROWS, :] = total


def pick(row, place):
    lane = lax.broadcasted_iota(jnp.int32, row.shape, 1)
    return jnp.sum(jnp.where(lane == place, row, 0.0)) > 0


def listed(row_ref, place):
    size = row_ref.shape[1]
    inside = (place >= 0) & (place < size)
    return inside & (row_ref[0, jnp.clip(place, 0, size - 1)] > 0)


def skeleton_rows(rank, dim):
    return (rank // LANES) * dim


def prepare(plan, near_row, iterate, points_t, basis, transfer, leaf_t, cluster_t):
    size = near_row.shape[1]
    n, half, dim = plan.n, plan.half, plan.dim
    rank = basis.shape[1]

    inputs = [points_t, iterate, near_row, leaf_t, cluster_t, basis, transfer]

    def kernel(*refs):
        count = len(inputs)
        sources, (pay_ref, down_ref, up_ref) = refs[:count], refs[count : count + 3]
        points_ref, iterate_ref, near_ref, leaf_ref, cluster_ref, basis_ref, transfer_ref, sems = refs[count + 3 :]
        copies = [
            pltpu.make_async_copy(source, into, sems.at[k])
            for k, (source, into) in enumerate(zip(sources, refs[count + 3 : -1]))
        ]
        for copy in copies:
            copy.start()
        copies[0].wait()
        for h in range(2):
            for b in range(plan.blocks):
                first = h * half + b * LANES
                pay_ref[h, half + b * dim : half + (b + 1) * dim, :] = (
                    2.0 * points_ref[:, first : first + LANES].astype(F32)
                ).astype(BF16)
        copies[1].wait()
        for h in range(2):
            pay_ref[h, 0:half, :] = iterate_ref[h * half : (h + 1) * half, :].astype(BF16)
        for copy in copies[2:]:
            copy.wait()
        lane = lax.broadcasted_iota(jnp.int32, (FLAG_ROWS, LANES), 1)
        row = jnp.zeros((FLAG_ROWS, LANES), F32)
        for k in range(size):
            row = jnp.where(lane == k, near_ref[0, k].astype(F32), row)
        for h in range(2):
            pay_ref[h, plan.flags :, :] = row.astype(BF16)

        def skeleton(ref, out_ref):
            doubled = doubled_of(ref)
            for b in range(rank // LANES):
                out_ref[rank + b * dim : rank + (b + 1) * dim, :] = doubled[:, b * LANES : (b + 1) * LANES]

        skeleton(leaf_ref, down_ref)
        skeleton(cluster_ref, up_ref)
        total = jnp.zeros((rank, plan.rhs), F32)
        for h in range(2):
            total = total + contract(
                basis_ref[h * half : (h + 1) * half, :], pay_ref[h, 0:half, :], ((0,), (0,))
            )
        coef = total.astype(BF16)
        down_ref[0:rank, :] = coef
        up_ref[0:rank, :] = contract(transfer_ref[0], coef, ((0,), (0,))).astype(BF16)

    rows = rank + skeleton_rows(rank, dim)
    return call(
        kernel,
        [plan.pay(), shaped(rows, plan.rhs), shaped(rows, plan.rhs)],
        [(pltpu.with_memory_space_constraint(value, HBM), HBM) for value in inputs],
        scratch=[(SMEM if value is near_row else VMEM)(value.shape, value.dtype) for value in inputs]
        + [pltpu.SemaphoreType.DMA((len(inputs),))],
        flops=2 * n * rank * plan.rhs,
    )


def own_tile(plan, pay):
    def kernel(pay_ref, acc_ref, left_ref, offset_ref):
        acc_ref[...] = jnp.zeros_like(acc_ref)
        for h in range(2):
            fill_left(plan, left_ref, pay_ref.at[h], h)

        @pl.loop(0, 2)
        def _(h):
            fill_offset(plan, offset_ref, pay_ref.at[h])
            half_tile(plan, acc_ref.at[0], left_ref, pay_ref.at[h], offset_ref)

    return call(
        kernel,
        plan.acc(),
        [(pay, VMEM)],
        scratch=[VMEM(plan.left().shape[1:], BF16)] + plan.offset_scratch(),
        flops=plan.tile_flops,
    )


def pair_tiles(plan, near_row, pay, partner, acc):
    def kernel(near_ref, pay_ref, partner_ref, acc_in, acc_ref, left_ref, row_ref, offset_ref):
        place = lax.axis_index("leaf")
        core = lax.rem(place, 2)
        for h in range(2):
            fill_left(plan, left_ref.at[0], pay_ref.at[h], h)
            fill_left(plan, left_ref.at[1], partner_ref.at[h], h)
        row = partner_ref[0, plan.flags :, :].astype(F32)
        row_ref[...] = row

        @pl.when(listed(near_ref, place + 1 - 2 * core))
        def _():
            fill_offset(plan, offset_ref, partner_ref.at[core])
            half_tile(plan, acc_ref.at[0], left_ref.at[0], partner_ref.at[core], offset_ref)

        @pl.when(pick(row, place))
        def _():
            fill_offset(plan, offset_ref, pay_ref.at[core])
            half_tile(plan, acc_ref.at[1], left_ref.at[1], pay_ref.at[core], offset_ref)

    return call(
        kernel,
        [plan.acc(), plan.left(), shaped(FLAG_ROWS, LANES, dtype=F32)],
        [(near_row, SMEM), (pay, VMEM), (partner, VMEM), (acc, VMEM)],
        scratch=plan.offset_scratch(),
        flops=plan.tile_flops,
        aliases={3: 0},
    )


def side_tiles(plan, near_row, row, left, full, passed, acc, reach, last):
    def kernel(near_ref, row_in, left_ref, full_ref, passed_ref, acc_in, acc_ref, *refs):
        offset_ref = refs[-1]
        place = lax.axis_index("leaf")
        core = lax.rem(place, 2)
        away = 2 * core - 1
        row = row_in[...]
        first = place + away * reach
        second = place - away - away * reach
        for source, at in ((full_ref.at[core], first), (passed_ref.at[core], second)):
            on_mine = listed(near_ref, at)
            on_theirs = pick(row, at)

            @pl.when(on_mine | on_theirs)
            def _():
                fill_offset(plan, offset_ref, source)

            @pl.loop(0, 2)
            def _(t):
                @pl.when(jnp.where(t == 0, on_mine, on_theirs))
                def _():
                    half_tile(plan, acc_ref.at[t], left_ref.at[t], source, offset_ref)

        if last:
            refs[0][...] = acc_ref[1]

    outs = [plan.acc()] + ([shaped(plan.n, plan.rhs, dtype=F32)] if last else [])
    return call(
        kernel,
        outs,
        [(near_row, SMEM), (row, VMEM), (left, VMEM), (full, VMEM), (passed, VMEM), (acc, VMEM)],
        scratch=plan.offset_scratch(),
        flops=2 * plan.tile_flops,
        aliases={5: 0},
    )


def wanted_rows(ordering, target):
    n, rhs = target.shape
    step = 2 * LANES

    def kernel(order_ref, target_hbm, out_ref, target_ref, halves_ref, sem):
        copy = pltpu.make_async_copy(target_hbm, target_ref, sem)
        copy.start()
        copy.wait()
        value = target_ref[...]
        high = value.astype(BF16)
        halves_ref[:, 0:rhs] = high
        halves_ref[:, rhs:] = (value - high.astype(F32)).astype(BF16)
        lane = lax.broadcasted_iota(jnp.int32, (LANES, LANES), 1).astype(F32)

        @pl.loop(0, n // step)
        def _(i):
            picks = []
            for k in range(step // LANES):
                rows = pl.ds(pl.multiple_of(i * step + k * LANES, LANES), LANES)
                index = jnp.broadcast_to(order_ref[:, rows].astype(F32), (LANES, LANES)).T
                picks.append(
                    jnp.concatenate(
                        [jnp.where(index == lane + c, 1.0, 0.0).astype(BF16) for c in range(0, n, LANES)], axis=1
                    )
                )
            both = matmul(jnp.concatenate(picks, axis=0), halves_ref[...])
            out_ref[pl.ds(pl.multiple_of(i * step, step), step), :] = both[:, 0:rhs] + both[:, rhs:]

    return call(
        kernel,
        shaped(n, rhs, dtype=F32),
        [(ordering, VMEM), (target, HBM)],
        scratch=[VMEM((n, rhs), F32), VMEM((n, 2 * rhs), BF16), pltpu.SemaphoreType.DMA],
        flops=n * n * 512,
    )


def last_tile(plan, near_row, pay, left, third, acc, returned, iterate, wanted, step_size, basis, local):
    def kernel(near_ref, pay_ref, left_ref, third_ref, acc_ref, returned_ref, iterate_ref, wanted_ref, step_ref, basis_ref, local_ref, out_hbm, out_ref, offset_ref, sems):
        place = lax.axis_index("leaf")
        away = 2 * lax.rem(place, 2) - 1
        out_ref[...] = acc_ref[0] + returned_ref[...]

        @pl.when(listed(near_ref, place + 3 * away))
        def _():
            @pl.loop(0, 2)
            def _(h):
                fill_offset(plan, offset_ref, third_ref.at[h])
                half_tile(plan, out_ref, left_ref.at[0], third_ref.at[h], offset_ref)

        copies = []
        for h in range(2):
            for b in range(plan.blocks):
                first = h * plan.half + b * LANES
                rows = slice(first, first + LANES)
                power = SHIFT - norms(doubled_block(plan, pay_ref.at[h], b))
                factor = jnp.exp2(jnp.broadcast_to(power, (LANES, LANES)).T)
                image = matmul(basis_ref[rows, :], local_ref[...]) + factor * out_ref[rows, :]
                out_ref[rows, :] = iterate_ref[rows, :] + step_ref[...] * (wanted_ref[rows, :] - image)
                if b % 4 == 3:
                    done = slice(first - 3 * LANES, first + LANES)
                    copies.append(
                        pltpu.make_async_copy(out_ref.at[done, :], out_hbm.at[done, :], sems.at[len(copies)])
                    )
                    copies[-1].start()
        for copy in copies:
            copy.wait()

    return call(
        kernel,
        shaped(plan.n, plan.rhs, dtype=F32),
        [
            (near_row, SMEM),
            (pay, VMEM),
            (left, VMEM),
            (third, VMEM),
            (acc, VMEM),
            (returned, VMEM),
            (iterate, VMEM),
            (wanted, VMEM),
            (step_size.reshape(1, -1), VMEM),
            (basis, VMEM),
            (local, VMEM),
        ],
        scratch=[VMEM((plan.n, plan.rhs), F32)]
        + plan.offset_scratch()
        + [pltpu.SemaphoreType.DMA((plan.n // (4 * LANES),))],
        into=HBM,
        flops=plan.tile_flops,
    )


def add_far(total, left, block_ref, first, rank, dim):
    right = jnp.concatenate(
        [
            extended(block_ref[first + rank + b * dim : first + rank + (b + 1) * dim, :], False).astype(BF16)
            for b in range(rank // LANES)
        ],
        axis=1,
    )
    return total + matmul(jnp.exp(matmul(left, right)).astype(BF16), block_ref[first : first + rank, :])


def across(cluster_row, cluster_t, own, others, distances, down_block):
    dim, rank = cluster_t.shape[1:]
    count = len(others)
    rows = down_block.shape[0]

    def kernel(far_ref, skeleton_ref, down_ref, own_ref, *refs):
        out_ref, total_ref = refs[count], refs[count + 1]
        me = lax.axis_index("group")
        left = small_left(doubled_of(skeleton_ref))
        total_ref[...] = jnp.zeros_like(total_ref)
        out_ref[0:rows, :] = down_ref[...]

        def include(at, block_ref):
            @pl.when(far_ref[0, at] > 0)
            def _():
                total_ref[...] = add_far(total_ref[...], left, block_ref, 0, rank, dim)

        include(me, own_ref)
        for k in range(count):
            include(distances(me, k), refs[k])
        out_ref[rows:, :] = total_ref[...].astype(BF16)

    return call(
        kernel,
        shaped(rows + rank, LANES),
        [(cluster_row, SMEM), (cluster_t, VMEM), (down_block, VMEM), (own, VMEM)] + [(o, VMEM) for o in others],
        scratch=[VMEM((rank, LANES), F32)],
        flops=2 * 4 * rank * rank * 512,
    )


def joined(mine, got, rank):
    rows = mine.shape[0] - rank

    def kernel(mine_ref, got_ref, out_ref):
        out_ref[0:rows, :] = mine_ref[0:rows, :]
        out_ref[rows : 2 * rows, :] = got_ref[0:rows, :]
        out_ref[2 * rows :, :] = (mine_ref[rows:, :].astype(F32) + got_ref[rows:, :].astype(F32)).astype(BF16)

    return call(kernel, shaped(2 * rows + rank, LANES), [(mine, VMEM), (got, VMEM)])


def down(far_row, leaf_t, transfer, mine, got, xors):
    dim, rank = leaf_t.shape[1:]
    rows = rank + skeleton_rows(rank, dim)
    count = (mine.shape[0] - rank) // rows

    def kernel(far_ref, skeleton_ref, transfer_ref, mine_ref, got_ref, out_ref, total_ref):
        place = lax.axis_index("leaf")
        left = small_left(doubled_of(skeleton_ref))
        lower = (mine_ref[count * rows :, :].astype(F32) + got_ref[count * rows :, :].astype(F32)).astype(BF16)
        total_ref[...] = matmul(transfer_ref[0], lower)
        for k, other in enumerate(xors):
            block_ref, at = (mine_ref, k) if k < count else (got_ref, k - count)

            @pl.when(far_ref[0, place ^ other] > 0)
            def _():
                total_ref[...] = add_far(total_ref[...], left, block_ref, at * rows, rank, dim)

        out_ref[...] = total_ref[...].astype(BF16)

    return call(
        kernel,
        shaped(rank, LANES),
        [(far_row, SMEM), (leaf_t, VMEM), (transfer, VMEM), (mine, VMEM), (got, VMEM)],
        scratch=[VMEM((rank, LANES), F32)],
        flops=2 * 8 * rank * rank * 512,
    )


def routed(block, axis, target):
    size = lax.axis_size(axis)
    route = [(i, target(i)) for i in range(size) if 0 <= target(i) < size]
    return lax.ppermute(block, axis, route)


def over_chips(i):
    return i + 2 - 4 * (i % 2)


def beside_chips(i):
    return i - 1 + 2 * (i % 2)


def on_chip(i):
    return i ^ 1


def body(
    points,
    ordering,
    iterate,
    target,
    step_size,
    leaf_basis,
    transfer,
    leaf_skeleton,
    cluster_skeleton,
    near_table,
    far_table,
    cluster_far,
):
    plan = Plan(points, iterate)
    leaves = lax.axis_size("leaf")
    groups = lax.axis_size("group")
    rank = leaf_basis.shape[1]
    leaf_t = jnp.swapaxes(leaf_skeleton, 1, 2)
    cluster_t = jnp.swapaxes(cluster_skeleton, 1, 2)

    pay, down_block, up_block = prepare(
        plan, near_table, iterate, points.T, leaf_basis, transfer, leaf_t, cluster_t
    )
    partner = routed(pay, "leaf", on_chip)
    over = routed(pay, "leaf", over_chips)
    others = [routed(up_block, "group", lambda i, k=k: i ^ k) for k in range(1, groups)]
    acc = own_tile(plan, pay)
    mine = across(cluster_far, cluster_t, up_block, others, lambda me, k: me ^ (k + 1), down_block)
    acc, left, row = pair_tiles(plan, near_table, pay, partner, acc)

    xors, bit = [0], leaves // 2
    while True:
        got = routed(mine, "leaf", lambda i, bit=bit: i ^ bit)
        xors = xors + [x ^ bit for x in xors]
        if bit == 1:
            break
        mine = joined(mine, got, rank)
        bit //= 2
    local = down(far_table, leaf_t, transfer, mine, got, xors)

    beside = routed(pay, "leaf", beside_chips)
    over_passed = routed(over, "leaf", on_chip)
    (acc,) = side_tiles(plan, near_table, row, left, over, over_passed, acc, 2, False)
    beside_passed = routed(beside, "leaf", on_chip)
    third = routed(beside, "leaf", over_chips)
    acc, theirs = side_tiles(plan, near_table, row, left, beside, beside_passed, acc, 1, True)
    returned = routed(theirs, "leaf", on_chip)
    wanted = wanted_rows(ordering, target)
    return last_tile(
        plan, near_table, pay, left, third, acc, returned, iterate, wanted, step_size, leaf_basis, local
    )


def solution(mesh):
    return jax.shard_map(
        body,
        mesh=mesh,
        in_specs=(
            P(("group", "leaf"), None),
            P(("group", "leaf"), None),
            P(("group", "leaf"), None),
            P(("group", "leaf"), None),
            P(),
            P(("group", "leaf"), None),
            P(("group", "leaf"), None, None),
            P(("group", "leaf"), None, None),
            P("group", None, None),
            P(("group", "leaf"), None),
            P(("group", "leaf"), None),
            P("group", None),
        ),
        out_specs=P(("group", "leaf"), None),
        check_vma=False,
    )
```

```python
import math

import jax
import jax.numpy as jnp
from jax import lax
from jax.experimental import pallas as pl
from jax.experimental.pallas import tpu as pltpu
from jax.sharding import PartitionSpec as P


LANES = 128
COLS = 256
ROWS = 1024
FLAG_ROWS = 16
SHIFT = 66.0
LOG2E = math.log2(math.e)
VMEM = pltpu.VMEM
SMEM = pltpu.SMEM
HBM = pltpu.HBM
F32 = jnp.float32
BF16 = jnp.bfloat16


def contract(left, right, dims):
    return lax.dot_general(left, right, (dims, ((), ())), preferred_element_type=F32)


def matmul(left, right):
    return contract(left, right, ((1,), (0,)))


def call(kernel, outs, ins, scratch=(), flops=0, limit=16, aliases=None, into=VMEM):
    single = not isinstance(outs, (list, tuple))
    shapes = [outs] if single else list(outs)
    results = pl.pallas_call(
        kernel,
        out_shape=shapes,
        in_specs=[pl.BlockSpec(memory_space=space) for _, space in ins],
        out_specs=[pl.BlockSpec(memory_space=into)] * len(shapes),
        scratch_shapes=list(scratch),
        input_output_aliases=aliases or {},
        compiler_params=pltpu.CompilerParams(vmem_limit_bytes=limit << 20),
        cost_estimate=pl.CostEstimate(
            flops=int(flops), bytes_accessed=sum(a.size * a.dtype.itemsize for a, _ in ins), transcendentals=0
        ),
    )(*[a for a, _ in ins])
    return results[0] if single else results


def shaped(*shape, dtype=BF16):
    return jax.ShapeDtypeStruct(shape, dtype)


class Plan:
    def __init__(self, points, iterate):
        self.n, self.dim = points.shape
        self.rhs = iterate.shape[1]
        self.half = self.n // 2
        self.blocks = self.half // LANES
        self.flags = self.half + self.blocks * self.dim
        self.rows = self.flags + FLAG_ROWS
        self.tile_flops = 2 * self.n * self.n * 512

    def pay(self):
        return shaped(2, self.rows, self.rhs)

    def acc(self):
        return shaped(2, self.n, self.rhs, dtype=F32)

    def left(self):
        return shaped(2, self.n, self.dim)

    def offset_scratch(self):
        return [VMEM((8, self.half), F32)]


def three_parts(value):
    high = value.astype(BF16).astype(F32)
    rest = value - high
    middle = rest.astype(BF16).astype(F32)
    return high, middle, rest - middle


def extended(doubled, left):
    dim, width = doubled.shape
    wide = doubled.astype(F32)
    parts = three_parts(-0.25 * jnp.sum(wide * wide, axis=0, keepdims=True))
    row = lax.broadcasted_iota(jnp.int32, (LANES - dim, width), 0)
    ones, first = (0, 3) if left else (3, 0)
    below = jnp.where((row >= ones) & (row < ones + 3), 1.0, 0.0)
    for k, part in enumerate(parts):
        below = jnp.where(row == first + k, part, below)
    return jnp.concatenate([0.5 * wide if left else wide, below], axis=0)


def small_left(doubled):
    width = doubled.shape[1]
    return jnp.concatenate(
        [extended(doubled[:, k : k + LANES], True).T.astype(BF16) for k in range(0, width, LANES)], axis=0
    )


def doubled_of(ref):
    return (2.0 * ref[0].astype(F32)).astype(BF16)


def left_block(doubled):
    twice = jnp.concatenate([doubled, doubled], axis=0).astype(F32)
    return (0.5 * twice.T)[:, 0 : doubled.shape[0]].astype(BF16)


def doubled_block(plan, ref, b):
    return ref[plan.half + b * plan.dim : plan.half + (b + 1) * plan.dim, :]


def fill_left(plan, out_ref, ref, h):
    for b in range(plan.blocks):
        first = h * plan.half + b * LANES
        out_ref[first : first + LANES, :] = left_block(doubled_block(plan, ref, b))


def norms(doubled):
    wide = doubled.astype(F32)
    return (0.25 * LOG2E) * jnp.sum(wide * wide, axis=0, keepdims=True)


def fill_offset(plan, offset_ref, ref):
    for b in range(plan.blocks):
        offset_ref[0:1, b * LANES : (b + 1) * LANES] = -norms(doubled_block(plan, ref, b)) - SHIFT


def half_tile(plan, acc_ref, left_ref, source_ref, offset_ref, beside=None):
    step = 0
    for r in range(0, plan.n, ROWS):
        left = left_ref[r : r + ROWS, :]
        total = acc_ref[r : r + ROWS, :]
        for c in range(0, plan.half, COLS):
            cols = slice(c, c + COLS)
            right = jnp.concatenate(
                [doubled_block(plan, source_ref, b) for b in range(c // LANES, (c + COLS) // LANES)], axis=1
            )
            power = matmul(left, right) * LOG2E + offset_ref[0:1, cols]
            total = total + matmul(jnp.exp2(power).astype(BF16), source_ref[cols, :])
            if beside is not None:
                beside(step)
            step += 1
        acc_ref[r : r + ROWS, :] = total


def pick(row, place):
    lane = lax.broadcasted_iota(jnp.int32, row.shape, 1)
    return jnp.sum(jnp.where(lane == place, row, 0.0)) > 0


def listed(row_ref, place):
    size = row_ref.shape[1]
    inside = (place >= 0) & (place < size)
    return inside & (row_ref[0, jnp.clip(place, 0, size - 1)] > 0)


def skeleton_rows(rank, dim):
    return (rank // LANES) * dim


def prepare(plan, near_row, iterate, points_t, basis, transfer, leaf_t, cluster_t):
    size = near_row.shape[1]
    n, half, dim = plan.n, plan.half, plan.dim
    rank = basis.shape[1]

    inputs = [points_t, iterate, near_row, leaf_t, cluster_t, basis, transfer]

    def kernel(*refs):
        count = len(inputs)
        sources, (pay_ref, down_ref, up_ref) = refs[:count], refs[count : count + 3]
        points_ref, iterate_ref, near_ref, leaf_ref, cluster_ref, basis_ref, transfer_ref, sems = refs[count + 3 :]
        copies = [
            pltpu.make_async_copy(source, into, sems.at[k])
            for k, (source, into) in enumerate(zip(sources, refs[count + 3 : -1]))
        ]
        for copy in copies:
            copy.start()
        copies[0].wait()
        for h in range(2):
            for b in range(plan.blocks):
                first = h * half + b * LANES
                pay_ref[h, half + b * dim : half + (b + 1) * dim, :] = (
                    2.0 * points_ref[:, first : first + LANES].astype(F32)
                ).astype(BF16)
        copies[1].wait()
        for h in range(2):
            pay_ref[h, 0:half, :] = iterate_ref[h * half : (h + 1) * half, :].astype(BF16)
        for copy in copies[2:]:
            copy.wait()
        lane = lax.broadcasted_iota(jnp.int32, (FLAG_ROWS, LANES), 1)
        row = jnp.zeros((FLAG_ROWS, LANES), F32)
        for k in range(size):
            row = jnp.where(lane == k, near_ref[0, k].astype(F32), row)
        for h in range(2):
            pay_ref[h, plan.flags :, :] = row.astype(BF16)

        def skeleton(ref, out_ref):
            doubled = doubled_of(ref)
            for b in range(rank // LANES):
                out_ref[rank + b * dim : rank + (b + 1) * dim, :] = doubled[:, b * LANES : (b + 1) * LANES]

        skeleton(leaf_ref, down_ref)
        skeleton(cluster_ref, up_ref)
        total = jnp.zeros((rank, plan.rhs), F32)
        for h in range(2):
            total = total + contract(
                basis_ref[h * half : (h + 1) * half, :], pay_ref[h, 0:half, :], ((0,), (0,))
            )
        coef = total.astype(BF16)
        down_ref[0:rank, :] = coef
        up_ref[0:rank, :] = contract(transfer_ref[0], coef, ((0,), (0,))).astype(BF16)

    rows = rank + skeleton_rows(rank, dim)
    return call(
        kernel,
        [plan.pay(), shaped(rows, plan.rhs), shaped(rows, plan.rhs)],
        [(pltpu.with_memory_space_constraint(value, HBM), HBM) for value in inputs],
        scratch=[(SMEM if value is near_row else VMEM)(value.shape, value.dtype) for value in inputs]
        + [pltpu.SemaphoreType.DMA((len(inputs),))],
        flops=2 * n * rank * plan.rhs,
    )


def own_tile(plan, pay, ordering, target):
    group = 8
    steps = (plan.n // ROWS) * (plan.half // COLS)

    def kernel(pay_ref, order_ref, target_ref, acc_ref, wanted_ref, left_ref, offset_ref):
        acc_ref[...] = jnp.zeros_like(acc_ref)
        for h in range(2):
            fill_left(plan, left_ref, pay_ref.at[h], h)

        @pl.loop(0, 2)
        def _(h):
            def gather(step):
                rows = plan.half // steps
                for k in range(step * rows, (step + 1) * rows, group):
                    first = pl.multiple_of(h * plan.half + k, group)
                    wanted_ref[pl.ds(first, group), :] = jnp.concatenate(
                        [target_ref[pl.ds(order_ref[0, first + u], 1), :] for u in range(group)], axis=0
                    )

            fill_offset(plan, offset_ref, pay_ref.at[h])
            half_tile(plan, acc_ref.at[0], left_ref, pay_ref.at[h], offset_ref, gather)

    return call(
        kernel,
        [plan.acc(), shaped(plan.n, plan.rhs, dtype=F32)],
        [(pay, VMEM), (ordering, SMEM), (target, VMEM)],
        scratch=[VMEM(plan.left().shape[1:], BF16)] + plan.offset_scratch(),
        flops=plan.tile_flops,
    )


def pair_tiles(plan, near_row, pay, partner, acc):
    def kernel(near_ref, pay_ref, partner_ref, acc_in, acc_ref, left_ref, row_ref, offset_ref):
        place = lax.axis_index("leaf")
        core = lax.rem(place, 2)
        for h in range(2):
            fill_left(plan, left_ref.at[0], pay_ref.at[h], h)
            fill_left(plan, left_ref.at[1], partner_ref.at[h], h)
        row = partner_ref[0, plan.flags :, :].astype(F32)
        row_ref[...] = row

        @pl.when(listed(near_ref, place + 1 - 2 * core))
        def _():
            fill_offset(plan, offset_ref, partner_ref.at[core])
            half_tile(plan, acc_ref.at[0], left_ref.at[0], partner_ref.at[core], offset_ref)

        @pl.when(pick(row, place))
        def _():
            fill_offset(plan, offset_ref, pay_ref.at[core])
            half_tile(plan, acc_ref.at[1], left_ref.at[1], pay_ref.at[core], offset_ref)

    return call(
        kernel,
        [plan.acc(), plan.left(), shaped(FLAG_ROWS, LANES, dtype=F32)],
        [(near_row, SMEM), (pay, VMEM), (partner, VMEM), (acc, VMEM)],
        scratch=plan.offset_scratch(),
        flops=plan.tile_flops,
        aliases={3: 0},
    )


def side_tiles(plan, near_row, row, left, full, passed, acc, reach, last):
    def kernel(near_ref, row_in, left_ref, full_ref, passed_ref, acc_in, acc_ref, *refs):
        offset_ref = refs[-1]
        place = lax.axis_index("leaf")
        core = lax.rem(place, 2)
        away = 2 * core - 1
        row = row_in[...]
        first = place + away * reach
        second = place - away - away * reach
        for source, at in ((full_ref.at[core], first), (passed_ref.at[core], second)):
            on_mine = listed(near_ref, at)
            on_theirs = pick(row, at)

            @pl.when(on_mine | on_theirs)
            def _():
                fill_offset(plan, offset_ref, source)

            @pl.loop(0, 2)
            def _(t):
                @pl.when(jnp.where(t == 0, on_mine, on_theirs))
                def _():
                    half_tile(plan, acc_ref.at[t], left_ref.at[t], source, offset_ref)

        if last:
            refs[0][...] = acc_ref[1].astype(BF16)

    outs = [plan.acc()] + ([shaped(plan.n, plan.rhs)] if last else [])
    return call(
        kernel,
        outs,
        [(near_row, SMEM), (row, VMEM), (left, VMEM), (full, VMEM), (passed, VMEM), (acc, VMEM)],
        scratch=plan.offset_scratch(),
        flops=2 * plan.tile_flops,
        aliases={5: 0},
    )


def last_tile(plan, near_row, pay, left, third, acc, returned, iterate, wanted, step_size, basis, local):
    def kernel(near_ref, pay_ref, left_ref, third_ref, acc_ref, returned_ref, iterate_ref, wanted_ref, step_ref, basis_ref, local_ref, out_hbm, out_ref, offset_ref, sems):
        place = lax.axis_index("leaf")
        away = 2 * lax.rem(place, 2) - 1
        out_ref[...] = acc_ref[0] + returned_ref[...].astype(F32)

        @pl.when(listed(near_ref, place + 3 * away))
        def _():
            @pl.loop(0, 2)
            def _(h):
                fill_offset(plan, offset_ref, third_ref.at[h])
                half_tile(plan, out_ref, left_ref.at[0], third_ref.at[h], offset_ref)

        copies = []
        for h in range(2):
            for b in range(plan.blocks):
                first = h * plan.half + b * LANES
                rows = slice(first, first + LANES)
                power = SHIFT - norms(doubled_block(plan, pay_ref.at[h], b))
                factor = jnp.exp2(jnp.broadcast_to(power, (LANES, LANES)).T)
                image = matmul(basis_ref[rows, :], local_ref[...]) + factor * out_ref[rows, :]
                out_ref[rows, :] = iterate_ref[rows, :] + step_ref[...] * (wanted_ref[rows, :] - image)
                if b % 4 == 3:
                    done = slice(first - 3 * LANES, first + LANES)
                    copies.append(
                        pltpu.make_async_copy(out_ref.at[done, :], out_hbm.at[done, :], sems.at[len(copies)])
                    )
                    copies[-1].start()
        for copy in copies:
            copy.wait()

    return call(
        kernel,
        shaped(plan.n, plan.rhs, dtype=F32),
        [
            (near_row, SMEM),
            (pay, VMEM),
            (left, VMEM),
            (third, VMEM),
            (acc, VMEM),
            (returned, VMEM),
            (iterate, VMEM),
            (wanted, VMEM),
            (step_size.reshape(1, -1), VMEM),
            (basis, VMEM),
            (local, VMEM),
        ],
        scratch=[VMEM((plan.n, plan.rhs), F32)]
        + plan.offset_scratch()
        + [pltpu.SemaphoreType.DMA((plan.n // (4 * LANES),))],
        into=HBM,
        flops=plan.tile_flops,
    )


def add_far(total, left, block_ref, first, rank, dim):
    right = jnp.concatenate(
        [
            extended(block_ref[first + rank + b * dim : first + rank + (b + 1) * dim, :], False).astype(BF16)
            for b in range(rank // LANES)
        ],
        axis=1,
    )
    return total + matmul(jnp.exp(matmul(left, right)).astype(BF16), block_ref[first : first + rank, :])


def across(cluster_row, cluster_t, own, others, distances, down_block):
    dim, rank = cluster_t.shape[1:]
    count = len(others)
    rows = down_block.shape[0]

    def kernel(far_ref, skeleton_ref, down_ref, own_ref, *refs):
        out_ref, total_ref = refs[count], refs[count + 1]
        me = lax.axis_index("group")
        left = small_left(doubled_of(skeleton_ref))
        total_ref[...] = jnp.zeros_like(total_ref)
        out_ref[0:rows, :] = down_ref[...]

        def include(at, block_ref):
            @pl.when(far_ref[0, at] > 0)
            def _():
                total_ref[...] = add_far(total_ref[...], left, block_ref, 0, rank, dim)

        include(me, own_ref)
        for k in range(count):
            include(distances(me, k), refs[k])
        out_ref[rows:, :] = total_ref[...].astype(BF16)

    return call(
        kernel,
        shaped(rows + rank, LANES),
        [(cluster_row, SMEM), (cluster_t, VMEM), (down_block, VMEM), (own, VMEM)] + [(o, VMEM) for o in others],
        scratch=[VMEM((rank, LANES), F32)],
        flops=2 * 4 * rank * rank * 512,
    )


def joined(mine, got, rank):
    rows = mine.shape[0] - rank
    count = 1 + len(got)

    def kernel(*refs):
        out_ref = refs[-1]
        share = jnp.zeros((rank, LANES), F32)
        for k, ref in enumerate(refs[:-1]):
            out_ref[k * rows : (k + 1) * rows, :] = ref[0:rows, :]
            share = share + ref[rows:, :].astype(F32)
        out_ref[count * rows :, :] = share.astype(BF16)

    return call(kernel, shaped(count * rows + rank, LANES), [(b, VMEM) for b in (mine, *got)])


def down(far_row, leaf_t, transfer, mine, got, xors):
    dim, rank = leaf_t.shape[1:]
    rows = rank + skeleton_rows(rank, dim)
    count = (mine.shape[0] - rank) // rows

    def kernel(far_ref, skeleton_ref, transfer_ref, mine_ref, got_ref, out_ref, total_ref):
        place = lax.axis_index("leaf")
        left = small_left(doubled_of(skeleton_ref))
        lower = (mine_ref[count * rows :, :].astype(F32) + got_ref[count * rows :, :].astype(F32)).astype(BF16)
        total_ref[...] = matmul(transfer_ref[0], lower)
        for k, other in enumerate(xors):
            block_ref, at = (mine_ref, k) if k < count else (got_ref, k - count)

            @pl.when(far_ref[0, place ^ other] > 0)
            def _():
                total_ref[...] = add_far(total_ref[...], left, block_ref, at * rows, rank, dim)

        out_ref[...] = total_ref[...].astype(BF16)

    return call(
        kernel,
        shaped(rank, LANES),
        [(far_row, SMEM), (leaf_t, VMEM), (transfer, VMEM), (mine, VMEM), (got, VMEM)],
        scratch=[VMEM((rank, LANES), F32)],
        flops=2 * 8 * rank * rank * 512,
    )


def routed(block, axis, target):
    size = lax.axis_size(axis)
    route = [(i, target(i)) for i in range(size) if 0 <= target(i) < size]
    return lax.ppermute(block, axis, route)


def over_chips(i):
    return i + 2 - 4 * (i % 2)


def beside_chips(i):
    return i - 1 + 2 * (i % 2)


def on_chip(i):
    return i ^ 1


def body(
    points,
    ordering,
    iterate,
    target,
    step_size,
    leaf_basis,
    transfer,
    leaf_skeleton,
    cluster_skeleton,
    near_table,
    far_table,
    cluster_far,
):
    plan = Plan(points, iterate)
    leaves = lax.axis_size("leaf")
    groups = lax.axis_size("group")
    rank = leaf_basis.shape[1]
    leaf_t = jnp.swapaxes(leaf_skeleton, 1, 2)
    cluster_t = jnp.swapaxes(cluster_skeleton, 1, 2)

    pay, down_block, up_block = prepare(
        plan, near_table, iterate, points.T, leaf_basis, transfer, leaf_t, cluster_t
    )
    partner = routed(pay, "leaf", on_chip)
    over = routed(pay, "leaf", over_chips)
    others = [routed(up_block, "group", lambda i, k=k: i ^ k) for k in range(1, groups)]
    acc, wanted = own_tile(plan, pay, ordering, target)
    mine = across(cluster_far, cluster_t, up_block, others, lambda me, k: me ^ (k + 1), down_block)
    acc, left, row = pair_tiles(plan, near_table, pay, partner, acc)

    even = list(range(2, leaves, 2))[::-1]
    blocks = [routed(mine, "leaf", lambda i, other=other: i ^ other) for other in even]
    mine = joined(mine, blocks, rank)
    got = routed(mine, "leaf", on_chip)
    xors = [0] + even
    xors = xors + [x ^ 1 for x in xors]
    local = down(far_table, leaf_t, transfer, mine, got, xors)

    beside = routed(pay, "leaf", beside_chips)
    over_passed = routed(over, "leaf", on_chip)
    (acc,) = side_tiles(plan, near_table, row, left, over, over_passed, acc, 2, False)
    beside_passed = routed(beside, "leaf", on_chip)
    third = routed(beside, "leaf", over_chips)
    acc, theirs = side_tiles(plan, near_table, row, left, beside, beside_passed, acc, 1, True)
    returned = routed(theirs, "leaf", on_chip)
    return last_tile(
        plan, near_table, pay, left, third, acc, returned, iterate, wanted, step_size, leaf_basis, local
    )


def solution(mesh):
    return jax.shard_map(
        body,
        mesh=mesh,
        in_specs=(
            P(("group", "leaf"), None),
            P(("group", "leaf"), None),
            P(("group", "leaf"), None),
            P(("group", "leaf"), None),
            P(),
            P(("group", "leaf"), None),
            P(("group", "leaf"), None, None),
            P(("group", "leaf"), None, None),
            P("group", None, None),
            P(("group", "leaf"), None),
            P(("group", "leaf"), None),
            P("group", None),
        ),
        out_specs=P(("group", "leaf"), None),
        check_vma=False,
    )
```

```python
import math

import jax
import jax.numpy as jnp
from jax import lax
from jax.experimental import pallas as pl
from jax.experimental.pallas import tpu as pltpu
from jax.sharding import PartitionSpec as P


LANES = 128
COLS = 256
ROWS = 1024
FLAG_ROWS = 16
SHIFT = 66.0
LOG2E = math.log2(math.e)
VMEM = pltpu.VMEM
SMEM = pltpu.SMEM
HBM = pltpu.HBM
F32 = jnp.float32
BF16 = jnp.bfloat16


def contract(left, right, dims):
    return lax.dot_general(left, right, (dims, ((), ())), preferred_element_type=F32)


def matmul(left, right):
    return contract(left, right, ((1,), (0,)))


def call(kernel, outs, ins, scratch=(), flops=0, limit=16, aliases=None, into=VMEM):
    single = not isinstance(outs, (list, tuple))
    shapes = [outs] if single else list(outs)
    results = pl.pallas_call(
        kernel,
        out_shape=shapes,
        in_specs=[pl.BlockSpec(memory_space=space) for _, space in ins],
        out_specs=[pl.BlockSpec(memory_space=into)] * len(shapes),
        scratch_shapes=list(scratch),
        input_output_aliases=aliases or {},
        compiler_params=pltpu.CompilerParams(vmem_limit_bytes=limit << 20),
        cost_estimate=pl.CostEstimate(
            flops=int(flops), bytes_accessed=sum(a.size * a.dtype.itemsize for a, _ in ins), transcendentals=0
        ),
    )(*[a for a, _ in ins])
    return results[0] if single else results


def shaped(*shape, dtype=BF16):
    return jax.ShapeDtypeStruct(shape, dtype)


class Plan:
    def __init__(self, points, iterate):
        self.n, self.dim = points.shape
        self.rhs = iterate.shape[1]
        self.half = self.n // 2
        self.blocks = self.half // LANES
        self.flags = self.half + self.blocks * self.dim
        self.rows = self.flags + FLAG_ROWS
        self.tile_flops = 2 * self.n * self.n * 512

    def pay(self):
        return shaped(2, self.rows, self.rhs)

    def acc(self):
        return shaped(2, self.n, self.rhs, dtype=F32)

    def left(self):
        return shaped(2, self.n, self.dim)

    def offset_scratch(self):
        return [VMEM((8, self.half), F32)]


def three_parts(value):
    high = value.astype(BF16).astype(F32)
    rest = value - high
    middle = rest.astype(BF16).astype(F32)
    return high, middle, rest - middle


def extended(doubled, left):
    dim, width = doubled.shape
    wide = doubled.astype(F32)
    parts = three_parts(-0.25 * jnp.sum(wide * wide, axis=0, keepdims=True))
    row = lax.broadcasted_iota(jnp.int32, (LANES - dim, width), 0)
    ones, first = (0, 3) if left else (3, 0)
    below = jnp.where((row >= ones) & (row < ones + 3), 1.0, 0.0)
    for k, part in enumerate(parts):
        below = jnp.where(row == first + k, part, below)
    return jnp.concatenate([0.5 * wide if left else wide, below], axis=0)


def small_left(doubled):
    width = doubled.shape[1]
    return jnp.concatenate(
        [extended(doubled[:, k : k + LANES], True).T.astype(BF16) for k in range(0, width, LANES)], axis=0
    )


def doubled_of(ref):
    return (2.0 * ref[0].astype(F32)).astype(BF16)


def left_block(doubled):
    twice = jnp.concatenate([doubled, doubled], axis=0).astype(F32)
    return (0.5 * twice.T)[:, 0 : doubled.shape[0]].astype(BF16)


def doubled_block(plan, ref, b):
    return ref[plan.half + b * plan.dim : plan.half + (b + 1) * plan.dim, :]


def fill_left(plan, out_ref, ref, h):
    for b in range(plan.blocks):
        first = h * plan.half + b * LANES
        out_ref[first : first + LANES, :] = left_block(doubled_block(plan, ref, b))


def norms(doubled):
    wide = doubled.astype(F32)
    return (0.25 * LOG2E) * jnp.sum(wide * wide, axis=0, keepdims=True)


def fill_offset(plan, offset_ref, ref):
    for b in range(plan.blocks):
        offset_ref[0:1, b * LANES : (b + 1) * LANES] = -norms(doubled_block(plan, ref, b)) - SHIFT


def half_tile(plan, acc_ref, left_ref, source_ref, offset_ref, beside=None):
    step = 0
    for r in range(0, plan.n, ROWS):
        left = left_ref[r : r + ROWS, :]
        total = acc_ref[r : r + ROWS, :]
        for c in range(0, plan.half, COLS):
            cols = slice(c, c + COLS)
            right = jnp.concatenate(
                [doubled_block(plan, source_ref, b) for b in range(c // LANES, (c + COLS) // LANES)], axis=1
            )
            power = matmul(left, right) * LOG2E + offset_ref[0:1, cols]
            total = total + matmul(jnp.exp2(power).astype(BF16), source_ref[cols, :])
            if beside is not None:
                beside(step)
            step += 1
        acc_ref[r : r + ROWS, :] = total


def pick(row, place):
    lane = lax.broadcasted_iota(jnp.int32, row.shape, 1)
    return jnp.sum(jnp.where(lane == place, row, 0.0)) > 0


def listed(row_ref, place):
    size = row_ref.shape[1]
    inside = (place >= 0) & (place < size)
    return inside & (row_ref[0, jnp.clip(place, 0, size - 1)] > 0)


def skeleton_rows(rank, dim):
    return (rank // LANES) * dim


def prepare(plan, near_row, iterate, points_t, basis, transfer, leaf_t, cluster_t):
    size = near_row.shape[1]
    n, half, dim = plan.n, plan.half, plan.dim
    rank = basis.shape[1]

    inputs = [points_t, iterate, near_row, leaf_t, cluster_t, basis, transfer]

    def kernel(*refs):
        count = len(inputs)
        sources, (pay_ref, down_ref, up_ref) = refs[:count], refs[count : count + 3]
        points_ref, iterate_ref, near_ref, leaf_ref, cluster_ref, basis_ref, transfer_ref, sems = refs[count + 3 :]
        copies = [
            pltpu.make_async_copy(source, into, sems.at[k])
            for k, (source, into) in enumerate(zip(sources, refs[count + 3 : -1]))
        ]
        for copy in copies:
            copy.start()
        copies[0].wait()
        for h in range(2):
            for b in range(plan.blocks):
                first = h * half + b * LANES
                pay_ref[h, half + b * dim : half + (b + 1) * dim, :] = (
                    2.0 * points_ref[:, first : first + LANES].astype(F32)
                ).astype(BF16)
        copies[1].wait()
        for h in range(2):
            pay_ref[h, 0:half, :] = iterate_ref[h * half : (h + 1) * half, :].astype(BF16)
        for copy in copies[2:]:
            copy.wait()
        lane = lax.broadcasted_iota(jnp.int32, (FLAG_ROWS, LANES), 1)
        row = jnp.zeros((FLAG_ROWS, LANES), F32)
        for k in range(size):
            row = jnp.where(lane == k, near_ref[0, k].astype(F32), row)
        for h in range(2):
            pay_ref[h, plan.flags :, :] = row.astype(BF16)

        def skeleton(ref, out_ref):
            doubled = doubled_of(ref)
            for b in range(rank // LANES):
                out_ref[rank + b * dim : rank + (b + 1) * dim, :] = doubled[:, b * LANES : (b + 1) * LANES]

        skeleton(leaf_ref, down_ref)
        skeleton(cluster_ref, up_ref)
        total = jnp.zeros((rank, plan.rhs), F32)
        for h in range(2):
            total = total + contract(
                basis_ref[h * half : (h + 1) * half, :], pay_ref[h, 0:half, :], ((0,), (0,))
            )
        coef = total.astype(BF16)
        down_ref[0:rank, :] = coef
        up_ref[0:rank, :] = contract(transfer_ref[0], coef, ((0,), (0,))).astype(BF16)

    rows = rank + skeleton_rows(rank, dim)
    return call(
        kernel,
        [plan.pay(), shaped(rows, plan.rhs), shaped(rows, plan.rhs)],
        [(pltpu.with_memory_space_constraint(value, HBM), HBM) for value in inputs],
        scratch=[(SMEM if value is near_row else VMEM)(value.shape, value.dtype) for value in inputs]
        + [pltpu.SemaphoreType.DMA((len(inputs),))],
        flops=2 * n * rank * plan.rhs,
    )


def own_tile(plan, pay, ordering, target, iterate, step_size):
    group = 8
    steps = (plan.n // ROWS) * (plan.half // COLS)
    rows = plan.half // steps

    def kernel(pay_ref, order_ref, target_ref, iterate_ref, step_ref, acc_ref, base_ref, factor_ref, left_ref, offset_ref):
        acc_ref[...] = jnp.zeros_like(acc_ref)
        for h in range(2):
            fill_left(plan, left_ref, pay_ref.at[h], h)
        step_row = step_ref[...]

        @pl.loop(0, 2)
        def _(h):
            def beside(step):
                for k in range(step * rows, (step + 1) * rows, group):
                    first = pl.multiple_of(h * plan.half + k, group)
                    here = pl.ds(first, group)
                    wanted = jnp.concatenate(
                        [target_ref[pl.ds(order_ref[0, first + u], 1), :] for u in range(group)], axis=0
                    )
                    base_ref[here, :] = iterate_ref[here, :] + step_row * wanted
                if (step * rows) % LANES == 0:
                    b = step * rows // LANES
                    here = pl.ds(pl.multiple_of(h * plan.half + b * LANES, LANES), LANES)
                    power = SHIFT + offset_ref[0:1, b * LANES : (b + 1) * LANES] + SHIFT
                    factor_ref[here, :] = step_row * jnp.exp2(jnp.broadcast_to(power, (LANES, LANES)).T)

            fill_offset(plan, offset_ref, pay_ref.at[h])
            half_tile(plan, acc_ref.at[0], left_ref, pay_ref.at[h], offset_ref, beside)

    full = shaped(plan.n, plan.rhs, dtype=F32)
    return call(
        kernel,
        [plan.acc(), full, full],
        [(pay, VMEM), (ordering, SMEM), (target, VMEM), (iterate, VMEM), (step_size, VMEM)],
        scratch=[VMEM(plan.left().shape[1:], BF16)] + plan.offset_scratch(),
        flops=plan.tile_flops,
    )


def pair_tiles(plan, near_row, pay, partner, acc):
    def kernel(near_ref, pay_ref, partner_ref, acc_in, acc_ref, left_ref, row_ref, offset_ref):
        place = lax.axis_index("leaf")
        core = lax.rem(place, 2)
        for h in range(2):
            fill_left(plan, left_ref.at[0], pay_ref.at[h], h)
            fill_left(plan, left_ref.at[1], partner_ref.at[h], h)
        row = partner_ref[0, plan.flags :, :].astype(F32)
        row_ref[...] = row

        @pl.when(listed(near_ref, place + 1 - 2 * core))
        def _():
            fill_offset(plan, offset_ref, partner_ref.at[core])
            half_tile(plan, acc_ref.at[0], left_ref.at[0], partner_ref.at[core], offset_ref)

        @pl.when(pick(row, place))
        def _():
            fill_offset(plan, offset_ref, pay_ref.at[core])
            half_tile(plan, acc_ref.at[1], left_ref.at[1], pay_ref.at[core], offset_ref)

    return call(
        kernel,
        [plan.acc(), plan.left(), shaped(FLAG_ROWS, LANES, dtype=F32)],
        [(near_row, SMEM), (pay, VMEM), (partner, VMEM), (acc, VMEM)],
        scratch=plan.offset_scratch(),
        flops=plan.tile_flops,
        aliases={3: 0},
    )


def side_tiles(plan, near_row, row, left, full, passed, acc, reach, last):
    def kernel(near_ref, row_in, left_ref, full_ref, passed_ref, acc_in, acc_ref, *refs):
        offset_ref = refs[-1]
        place = lax.axis_index("leaf")
        core = lax.rem(place, 2)
        away = 2 * core - 1
        row = row_in[...]
        first = place + away * reach
        second = place - away - away * reach
        for source, at in ((full_ref.at[core], first), (passed_ref.at[core], second)):
            on_mine = listed(near_ref, at)
            on_theirs = pick(row, at)

            @pl.when(on_mine | on_theirs)
            def _():
                fill_offset(plan, offset_ref, source)

            @pl.loop(0, 2)
            def _(t):
                @pl.when(jnp.where(t == 0, on_mine, on_theirs))
                def _():
                    half_tile(plan, acc_ref.at[t], left_ref.at[t], source, offset_ref)

        if last:
            refs[0][...] = acc_ref[1].astype(BF16)

    outs = [plan.acc()] + ([shaped(plan.n, plan.rhs)] if last else [])
    return call(
        kernel,
        outs,
        [(near_row, SMEM), (row, VMEM), (left, VMEM), (full, VMEM), (passed, VMEM), (acc, VMEM)],
        scratch=plan.offset_scratch(),
        flops=2 * plan.tile_flops,
        aliases={5: 0},
    )


def third_tile(plan, near_row, left, third, acc):
    def kernel(near_ref, left_ref, third_ref, acc_in, acc_ref, offset_ref):
        place = lax.axis_index("leaf")
        away = 2 * lax.rem(place, 2) - 1

        @pl.when(listed(near_ref, place + 3 * away))
        def _():
            @pl.loop(0, 2)
            def _(h):
                fill_offset(plan, offset_ref, third_ref.at[h])
                half_tile(plan, acc_ref.at[0], left_ref.at[0], third_ref.at[h], offset_ref)

    return call(
        kernel,
        plan.acc(),
        [(near_row, SMEM), (left, VMEM), (third, VMEM), (acc, VMEM)],
        scratch=plan.offset_scratch(),
        flops=plan.tile_flops,
        aliases={3: 0},
    )


def finish(plan, acc, returned, base, factor, step_size, basis, local):
    piece = 4 * LANES

    def kernel(acc_ref, returned_ref, base_ref, factor_ref, step_ref, basis_ref, local_ref, out_hbm, out_ref, sems):
        copies = []
        for first in range(0, plan.n, piece):
            rows = slice(first, first + piece)
            far = step_ref[...] * matmul(basis_ref[rows, :], local_ref[...])
            near = factor_ref[rows, :] * (acc_ref[0, rows, :] + returned_ref[rows, :].astype(F32))
            out_ref[rows, :] = base_ref[rows, :] - (far + near)
            copies.append(pltpu.make_async_copy(out_ref.at[rows, :], out_hbm.at[rows, :], sems.at[len(copies)]))
            copies[-1].start()
        for copy in copies:
            copy.wait()

    return call(
        kernel,
        shaped(plan.n, plan.rhs, dtype=F32),
        [(value, VMEM) for value in (acc, returned, base, factor, step_size, basis, local)],
        scratch=[VMEM((plan.n, plan.rhs), F32), pltpu.SemaphoreType.DMA((plan.n // piece,))],
        into=HBM,
        flops=2 * plan.n * basis.shape[1] * plan.rhs,
    )


def add_far(total, left, block_ref, first, rank, dim):
    right = jnp.concatenate(
        [
            extended(block_ref[first + rank + b * dim : first + rank + (b + 1) * dim, :], False).astype(BF16)
            for b in range(rank // LANES)
        ],
        axis=1,
    )
    return total + matmul(jnp.exp(matmul(left, right)).astype(BF16), block_ref[first : first + rank, :])


def across(cluster_row, cluster_t, own, others, distances, down_block):
    dim, rank = cluster_t.shape[1:]
    count = len(others)
    rows = down_block.shape[0]

    def kernel(far_ref, skeleton_ref, down_ref, own_ref, *refs):
        out_ref, total_ref = refs[count], refs[count + 1]
        me = lax.axis_index("group")
        left = small_left(doubled_of(skeleton_ref))
        total_ref[...] = jnp.zeros_like(total_ref)
        out_ref[0:rows, :] = down_ref[...]

        def include(at, block_ref):
            @pl.when(far_ref[0, at] > 0)
            def _():
                total_ref[...] = add_far(total_ref[...], left, block_ref, 0, rank, dim)

        include(me, own_ref)
        for k in range(count):
            include(distances(me, k), refs[k])
        out_ref[rows:, :] = total_ref[...].astype(BF16)

    return call(
        kernel,
        shaped(rows + rank, LANES),
        [(cluster_row, SMEM), (cluster_t, VMEM), (down_block, VMEM), (own, VMEM)] + [(o, VMEM) for o in others],
        scratch=[VMEM((rank, LANES), F32)],
        flops=2 * 4 * rank * rank * 512,
    )


def joined(mine, got, rank):
    rows = mine.shape[0] - rank
    count = 1 + len(got)

    def kernel(*refs):
        out_ref = refs[-1]
        share = jnp.zeros((rank, LANES), F32)
        for k, ref in enumerate(refs[:-1]):
            out_ref[k * rows : (k + 1) * rows, :] = ref[0:rows, :]
            share = share + ref[rows:, :].astype(F32)
        out_ref[count * rows :, :] = share.astype(BF16)

    return call(kernel, shaped(count * rows + rank, LANES), [(b, VMEM) for b in (mine, *got)])


def down(far_row, leaf_t, transfer, mine, got, xors):
    dim, rank = leaf_t.shape[1:]
    rows = rank + skeleton_rows(rank, dim)
    count = (mine.shape[0] - rank) // rows

    def kernel(far_ref, skeleton_ref, transfer_ref, mine_ref, got_ref, out_ref, total_ref):
        place = lax.axis_index("leaf")
        left = small_left(doubled_of(skeleton_ref))
        lower = (mine_ref[count * rows :, :].astype(F32) + got_ref[count * rows :, :].astype(F32)).astype(BF16)
        total_ref[...] = matmul(transfer_ref[0], lower)
        for k, other in enumerate(xors):
            block_ref, at = (mine_ref, k) if k < count else (got_ref, k - count)

            @pl.when(far_ref[0, place ^ other] > 0)
            def _():
                total_ref[...] = add_far(total_ref[...], left, block_ref, at * rows, rank, dim)

        out_ref[...] = total_ref[...].astype(BF16)

    return call(
        kernel,
        shaped(rank, LANES),
        [(far_row, SMEM), (leaf_t, VMEM), (transfer, VMEM), (mine, VMEM), (got, VMEM)],
        scratch=[VMEM((rank, LANES), F32)],
        flops=2 * 8 * rank * rank * 512,
    )


def routed(block, axis, target):
    size = lax.axis_size(axis)
    route = [(i, target(i)) for i in range(size) if 0 <= target(i) < size]
    return lax.ppermute(block, axis, route)


def over_chips(i):
    return i + 2 - 4 * (i % 2)


def beside_chips(i):
    return i - 1 + 2 * (i % 2)


def on_chip(i):
    return i ^ 1


def body(
    points,
    ordering,
    iterate,
    target,
    step_size,
    leaf_basis,
    transfer,
    leaf_skeleton,
    cluster_skeleton,
    near_table,
    far_table,
    cluster_far,
):
    plan = Plan(points, iterate)
    leaves = lax.axis_size("leaf")
    groups = lax.axis_size("group")
    rank = leaf_basis.shape[1]
    leaf_t = jnp.swapaxes(leaf_skeleton, 1, 2)
    cluster_t = jnp.swapaxes(cluster_skeleton, 1, 2)

    pay, down_block, up_block = prepare(
        plan, near_table, iterate, points.T, leaf_basis, transfer, leaf_t, cluster_t
    )
    partner = routed(pay, "leaf", on_chip)
    over = routed(pay, "leaf", over_chips)
    others = [routed(up_block, "group", lambda i, k=k: i ^ k) for k in range(1, groups)]
    step_row = step_size.reshape(1, -1)
    acc, base, factor = own_tile(plan, pay, ordering, target, iterate, step_row)
    mine = across(cluster_far, cluster_t, up_block, others, lambda me, k: me ^ (k + 1), down_block)
    acc, left, row = pair_tiles(plan, near_table, pay, partner, acc)

    even = list(range(2, leaves, 2))[::-1]
    blocks = [routed(mine, "leaf", lambda i, other=other: i ^ other) for other in even]
    mine = joined(mine, blocks, rank)
    got = routed(mine, "leaf", on_chip)
    xors = [0] + even
    xors = xors + [x ^ 1 for x in xors]
    local = down(far_table, leaf_t, transfer, mine, got, xors)

    beside = routed(pay, "leaf", beside_chips)
    over_passed = routed(over, "leaf", on_chip)
    (acc,) = side_tiles(plan, near_table, row, left, over, over_passed, acc, 2, False)
    beside_passed = routed(beside, "leaf", on_chip)
    third = routed(beside, "leaf", over_chips)
    acc, theirs = side_tiles(plan, near_table, row, left, beside, beside_passed, acc, 1, True)
    returned = routed(theirs, "leaf", on_chip)
    acc = third_tile(plan, near_table, left, third, acc)
    return finish(plan, acc, returned, base, factor, step_row, leaf_basis, local)


def solution(mesh):
    return jax.shard_map(
        body,
        mesh=mesh,
        in_specs=(
            P(("group", "leaf"), None),
            P(("group", "leaf"), None),
            P(("group", "leaf"), None),
            P(("group", "leaf"), None),
            P(),
            P(("group", "leaf"), None),
            P(("group", "leaf"), None, None),
            P(("group", "leaf"), None, None),
            P("group", None, None),
            P(("group", "leaf"), None),
            P(("group", "leaf"), None),
            P("group", None),
        ),
        out_specs=P(("group", "leaf"), None),
        check_vma=False,
    )
```

```python
import math

import jax
import jax.numpy as jnp
from jax import lax
from jax.experimental import pallas as pl
from jax.experimental.pallas import tpu as pltpu
from jax.sharding import PartitionSpec as P


LANES = 128
COLS = 256
ROWS = 1024
FLAG_ROWS = 16
SHIFT = 66.0
LOG2E = math.log2(math.e)
VMEM = pltpu.VMEM
SMEM = pltpu.SMEM
HBM = pltpu.HBM
F32 = jnp.float32
BF16 = jnp.bfloat16


def contract(left, right, dims):
    return lax.dot_general(left, right, (dims, ((), ())), preferred_element_type=F32)


def matmul(left, right):
    return contract(left, right, ((1,), (0,)))


def call(kernel, outs, ins, scratch=(), flops=0, limit=16, aliases=None, into=VMEM):
    single = not isinstance(outs, (list, tuple))
    shapes = [outs] if single else list(outs)
    results = pl.pallas_call(
        kernel,
        out_shape=shapes,
        in_specs=[pl.BlockSpec(memory_space=space) for _, space in ins],
        out_specs=[pl.BlockSpec(memory_space=into)] * len(shapes),
        scratch_shapes=list(scratch),
        input_output_aliases=aliases or {},
        compiler_params=pltpu.CompilerParams(vmem_limit_bytes=limit << 20),
        cost_estimate=pl.CostEstimate(
            flops=int(flops), bytes_accessed=sum(a.size * a.dtype.itemsize for a, _ in ins), transcendentals=0
        ),
    )(*[a for a, _ in ins])
    return results[0] if single else results


def shaped(*shape, dtype=BF16):
    return jax.ShapeDtypeStruct(shape, dtype)


class Plan:
    def __init__(self, points, iterate):
        self.n, self.dim = points.shape
        self.rhs = iterate.shape[1]
        self.half = self.n // 2
        self.blocks = self.half // LANES
        self.flags = self.half + self.blocks * self.dim
        self.rows = self.flags + FLAG_ROWS
        self.tile_flops = 2 * self.n * self.n * 512

    def pay(self):
        return shaped(2, self.rows, self.rhs)

    def acc(self):
        return shaped(2, self.n, self.rhs, dtype=F32)

    def left(self):
        return shaped(2, self.n, self.dim)

    def offset_scratch(self):
        return [VMEM((8, self.half), F32)]


def three_parts(value):
    high = value.astype(BF16).astype(F32)
    rest = value - high
    middle = rest.astype(BF16).astype(F32)
    return high, middle, rest - middle


def extended(doubled, left):
    dim, width = doubled.shape
    wide = doubled.astype(F32)
    parts = three_parts(-0.25 * jnp.sum(wide * wide, axis=0, keepdims=True))
    row = lax.broadcasted_iota(jnp.int32, (LANES - dim, width), 0)
    ones, first = (0, 3) if left else (3, 0)
    below = jnp.where((row >= ones) & (row < ones + 3), 1.0, 0.0)
    for k, part in enumerate(parts):
        below = jnp.where(row == first + k, part, below)
    return jnp.concatenate([0.5 * wide if left else wide, below], axis=0)


def small_left(doubled):
    width = doubled.shape[1]
    return jnp.concatenate(
        [extended(doubled[:, k : k + LANES], True).T.astype(BF16) for k in range(0, width, LANES)], axis=0
    )


def doubled_of(ref):
    return (2.0 * ref[0].astype(F32)).astype(BF16)


def left_block(doubled):
    twice = jnp.concatenate([doubled, doubled], axis=0).astype(F32)
    return (0.5 * twice.T)[:, 0 : doubled.shape[0]].astype(BF16)


def doubled_block(plan, ref, b):
    return ref[plan.half + b * plan.dim : plan.half + (b + 1) * plan.dim, :]


def fill_left(plan, out_ref, ref, h):
    for b in range(plan.blocks):
        first = h * plan.half + b * LANES
        out_ref[first : first + LANES, :] = left_block(doubled_block(plan, ref, b))


def norms(doubled):
    wide = doubled.astype(F32)
    return (0.25 * LOG2E) * jnp.sum(wide * wide, axis=0, keepdims=True)


def fill_offset(plan, offset_ref, ref):
    for b in range(plan.blocks):
        offset_ref[0:1, b * LANES : (b + 1) * LANES] = -norms(doubled_block(plan, ref, b)) - SHIFT


def half_tile(plan, acc_ref, left_ref, source_ref, offset_ref, beside=None):
    step = 0
    for r in range(0, plan.n, ROWS):
        left = left_ref[r : r + ROWS, :]
        total = acc_ref[r : r + ROWS, :]
        for c in range(0, plan.half, COLS):
            cols = slice(c, c + COLS)
            right = jnp.concatenate(
                [doubled_block(plan, source_ref, b) for b in range(c // LANES, (c + COLS) // LANES)], axis=1
            )
            power = matmul(left, right) * LOG2E + offset_ref[0:1, cols]
            total = total + matmul(jnp.exp2(power).astype(BF16), source_ref[cols, :])
            if beside is not None:
                beside(step)
            step += 1
        acc_ref[r : r + ROWS, :] = total


def pick(row, place):
    lane = lax.broadcasted_iota(jnp.int32, row.shape, 1)
    return jnp.sum(jnp.where(lane == place, row, 0.0)) > 0


def skeleton_rows(rank, dim):
    return (rank // LANES) * dim


def prepare(plan, near_row, iterate, points_t, basis, transfer, leaf_t, cluster_t):
    size = near_row.shape[1]
    n, half, dim = plan.n, plan.half, plan.dim
    rank = basis.shape[1]

    inputs = [points_t, iterate, near_row, leaf_t, cluster_t, basis, transfer]

    def kernel(*refs):
        count = len(inputs)
        sources, (pay_ref, down_ref, up_ref) = refs[:count], refs[count : count + 3]
        points_ref, iterate_ref, near_ref, leaf_ref, cluster_ref, basis_ref, transfer_ref, sems = refs[count + 3 :]
        copies = [
            pltpu.make_async_copy(source, into, sems.at[k])
            for k, (source, into) in enumerate(zip(sources, refs[count + 3 : -1]))
        ]
        for copy in copies:
            copy.start()
        copies[0].wait()
        for h in range(2):
            for b in range(plan.blocks):
                first = h * half + b * LANES
                pay_ref[h, half + b * dim : half + (b + 1) * dim, :] = (
                    2.0 * points_ref[:, first : first + LANES].astype(F32)
                ).astype(BF16)
        copies[1].wait()
        for h in range(2):
            pay_ref[h, 0:half, :] = iterate_ref[h * half : (h + 1) * half, :].astype(BF16)
        for copy in copies[2:]:
            copy.wait()
        lane = lax.broadcasted_iota(jnp.int32, (FLAG_ROWS, LANES), 1)
        row = jnp.zeros((FLAG_ROWS, LANES), F32)
        for k in range(size):
            row = jnp.where(lane == k, near_ref[0, k].astype(F32), row)
        for h in range(2):
            pay_ref[h, plan.flags :, :] = row.astype(BF16)

        def skeleton(ref, out_ref):
            doubled = doubled_of(ref)
            for b in range(rank // LANES):
                out_ref[rank + b * dim : rank + (b + 1) * dim, :] = doubled[:, b * LANES : (b + 1) * LANES]

        skeleton(leaf_ref, down_ref)
        skeleton(cluster_ref, up_ref)
        total = jnp.zeros((rank, plan.rhs), F32)
        for h in range(2):
            total = total + contract(
                basis_ref[h * half : (h + 1) * half, :], pay_ref[h, 0:half, :], ((0,), (0,))
            )
        coef = total.astype(BF16)
        down_ref[0:rank, :] = coef
        up_ref[0:rank, :] = contract(transfer_ref[0], coef, ((0,), (0,))).astype(BF16)

    rows = rank + skeleton_rows(rank, dim)
    return call(
        kernel,
        [plan.pay(), shaped(rows, plan.rhs), shaped(rows, plan.rhs)],
        [(pltpu.with_memory_space_constraint(value, HBM), HBM) for value in inputs],
        scratch=[(SMEM if value is near_row else VMEM)(value.shape, value.dtype) for value in inputs]
        + [pltpu.SemaphoreType.DMA((len(inputs),))],
        flops=2 * n * rank * plan.rhs,
    )


def own_tile(plan, pay, ordering, target, iterate, step_size):
    group = 8
    steps = (plan.n // ROWS) * (plan.half // COLS)
    rows = plan.half // steps

    def kernel(pay_ref, order_ref, target_ref, iterate_ref, step_ref, acc_ref, base_ref, left_ref, offset_ref):
        acc_ref[...] = jnp.zeros_like(acc_ref)
        for h in range(2):
            fill_left(plan, left_ref, pay_ref.at[h], h)
        step_row = step_ref[...]

        @pl.loop(0, 2)
        def _(h):
            def beside(step):
                for k in range(step * rows, (step + 1) * rows, group):
                    first = pl.multiple_of(h * plan.half + k, group)
                    here = pl.ds(first, group)
                    wanted = jnp.concatenate(
                        [target_ref[pl.ds(order_ref[0, first + u], 1), :] for u in range(group)], axis=0
                    )
                    base_ref[here, :] = iterate_ref[here, :] + step_row * wanted

            fill_offset(plan, offset_ref, pay_ref.at[h])
            half_tile(plan, acc_ref.at[0], left_ref, pay_ref.at[h], offset_ref, beside)

    full = shaped(plan.n, plan.rhs, dtype=F32)
    return call(
        kernel,
        [plan.acc(), full],
        [(pay, VMEM), (ordering, SMEM), (target, VMEM), (iterate, VMEM), (step_size, VMEM)],
        scratch=[VMEM(plan.left().shape[1:], BF16)] + plan.offset_scratch(),
        flops=plan.tile_flops,
    )


def pair_tiles(plan, pay, partner, acc):
    def kernel(pay_ref, partner_ref, acc_in, acc_ref, left_ref, row_ref, offset_ref):
        place = lax.axis_index("leaf")
        core = lax.rem(place, 2)
        for h in range(2):
            fill_left(plan, left_ref.at[0], pay_ref.at[h], h)
            fill_left(plan, left_ref.at[1], partner_ref.at[h], h)
        rows = [ref[0, plan.flags :, :].astype(F32) for ref in (pay_ref, partner_ref)]
        for t in range(2):
            row_ref[t] = rows[t][0:8, :]

        @pl.when(pick(rows[0][0:8, :], place + 1 - 2 * core))
        def _():
            fill_offset(plan, offset_ref, partner_ref.at[core])
            half_tile(plan, acc_ref.at[0], left_ref.at[0], partner_ref.at[core], offset_ref)

        @pl.when(pick(rows[1][0:8, :], place))
        def _():
            fill_offset(plan, offset_ref, pay_ref.at[core])
            half_tile(plan, acc_ref.at[1], left_ref.at[1], pay_ref.at[core], offset_ref)

    return call(
        kernel,
        [plan.acc(), plan.left(), shaped(2, 8, LANES, dtype=F32)],
        [(pay, VMEM), (partner, VMEM), (acc, VMEM)],
        scratch=plan.offset_scratch(),
        flops=plan.tile_flops,
        aliases={2: 0},
    )


def side_tiles(plan, row, left, full, passed, acc, reach, last):
    def kernel(row_ref, left_ref, full_ref, passed_ref, acc_in, acc_ref, *refs):
        offset_ref = refs[-1]
        place = lax.axis_index("leaf")
        core = lax.rem(place, 2)
        away = 2 * core - 1
        first = place + away * reach
        second = place - away - away * reach
        for source, at in ((full_ref.at[core], first), (passed_ref.at[core], second)):
            on_mine = pick(row_ref[0], at)
            on_theirs = pick(row_ref[1], at)

            @pl.when(on_mine | on_theirs)
            def _():
                fill_offset(plan, offset_ref, source)

            @pl.loop(0, 2)
            def _(t):
                @pl.when(jnp.where(t == 0, on_mine, on_theirs))
                def _():
                    half_tile(plan, acc_ref.at[t], left_ref.at[t], source, offset_ref)

        if last:
            refs[0][...] = acc_ref[1].astype(BF16)

    outs = [plan.acc()] + ([shaped(plan.n, plan.rhs)] if last else [])
    return call(
        kernel,
        outs,
        [(row, VMEM), (left, VMEM), (full, VMEM), (passed, VMEM), (acc, VMEM)],
        scratch=plan.offset_scratch(),
        flops=2 * plan.tile_flops,
        aliases={4: 0},
    )


def third_tile(plan, row, left, third, acc):
    def kernel(row_ref, left_ref, third_ref, acc_in, acc_ref, offset_ref):
        place = lax.axis_index("leaf")
        away = 2 * lax.rem(place, 2) - 1

        @pl.when(pick(row_ref[0], place + 3 * away))
        def _():
            @pl.loop(0, 2)
            def _(h):
                fill_offset(plan, offset_ref, third_ref.at[h])
                half_tile(plan, acc_ref.at[0], left_ref.at[0], third_ref.at[h], offset_ref)

    return call(
        kernel,
        plan.acc(),
        [(row, VMEM), (left, VMEM), (third, VMEM), (acc, VMEM)],
        scratch=plan.offset_scratch(),
        flops=plan.tile_flops,
        aliases={3: 0},
    )


def finish(plan, pay, acc, returned, base, step_size, basis, local):
    piece = 4 * LANES

    def kernel(pay_ref, acc_ref, returned_ref, base_ref, step_ref, basis_ref, local_ref, out_hbm, out_ref, sems):
        copies = []
        for first in range(0, plan.n, piece):
            rows = slice(first, first + piece)
            far = matmul(basis_ref[rows, :], local_ref[...])
            near = acc_ref[0, rows, :] + returned_ref[rows, :].astype(F32)
            powers = [
                SHIFT - norms(doubled_block(plan, pay_ref.at[at // plan.half], at % plan.half // LANES))
                for at in range(first, first + piece, LANES)
            ]
            factor = jnp.concatenate([jnp.exp2(jnp.broadcast_to(p, (LANES, LANES)).T) for p in powers], axis=0)
            out_ref[rows, :] = base_ref[rows, :] - step_ref[...] * (far + factor * near)
            copies.append(pltpu.make_async_copy(out_ref.at[rows, :], out_hbm.at[rows, :], sems.at[len(copies)]))
            copies[-1].start()
        for copy in copies:
            copy.wait()

    return call(
        kernel,
        shaped(plan.n, plan.rhs, dtype=F32),
        [(value, VMEM) for value in (pay, acc, returned, base, step_size, basis, local)],
        scratch=[VMEM((plan.n, plan.rhs), F32), pltpu.SemaphoreType.DMA((plan.n // piece,))],
        into=HBM,
        flops=2 * plan.n * basis.shape[1] * plan.rhs,
    )


def add_far(total, left, block_ref, first, rank, dim):
    right = jnp.concatenate(
        [
            extended(block_ref[first + rank + b * dim : first + rank + (b + 1) * dim, :], False).astype(BF16)
            for b in range(rank // LANES)
        ],
        axis=1,
    )
    return total + matmul(jnp.exp(matmul(left, right)).astype(BF16), block_ref[first : first + rank, :])


def across(cluster_row, cluster_t, own, others, distances, down_block):
    dim, rank = cluster_t.shape[1:]
    count = len(others)
    rows = down_block.shape[0]

    def kernel(far_ref, skeleton_ref, down_ref, own_ref, *refs):
        out_ref, total_ref = refs[count], refs[count + 1]
        me = lax.axis_index("group")
        left = small_left(doubled_of(skeleton_ref))
        total_ref[...] = jnp.zeros_like(total_ref)
        out_ref[0:rows, :] = down_ref[...]

        def include(at, block_ref):
            @pl.when(far_ref[0, at] > 0)
            def _():
                total_ref[...] = add_far(total_ref[...], left, block_ref, 0, rank, dim)

        include(me, own_ref)
        for k in range(count):
            include(distances(me, k), refs[k])
        out_ref[rows:, :] = total_ref[...].astype(BF16)

    return call(
        kernel,
        shaped(rows + rank, LANES),
        [(cluster_row, SMEM), (cluster_t, VMEM), (down_block, VMEM), (own, VMEM)] + [(o, VMEM) for o in others],
        scratch=[VMEM((rank, LANES), F32)],
        flops=2 * 4 * rank * rank * 512,
    )


def joined(mine, got, rank):
    rows = mine.shape[0] - rank

    def kernel(mine_ref, got_ref, out_ref):
        out_ref[0:rows, :] = mine_ref[0:rows, :]
        out_ref[rows : 2 * rows, :] = got_ref[0:rows, :]
        out_ref[2 * rows :, :] = (mine_ref[rows:, :].astype(F32) + got_ref[rows:, :].astype(F32)).astype(BF16)

    return call(kernel, shaped(2 * rows + rank, LANES), [(mine, VMEM), (got, VMEM)])


def down(far_row, leaf_t, transfer, mine, got, xors):
    dim, rank = leaf_t.shape[1:]
    rows = rank + skeleton_rows(rank, dim)
    count = (mine.shape[0] - rank) // rows

    def kernel(far_ref, skeleton_ref, transfer_ref, mine_ref, got_ref, out_ref, total_ref):
        place = lax.axis_index("leaf")
        left = small_left(doubled_of(skeleton_ref))
        lower = (mine_ref[count * rows :, :].astype(F32) + got_ref[count * rows :, :].astype(F32)).astype(BF16)
        total_ref[...] = matmul(transfer_ref[0], lower)
        for k, other in enumerate(xors):
            block_ref, at = (mine_ref, k) if k < count else (got_ref, k - count)

            @pl.when(far_ref[0, place ^ other] > 0)
            def _():
                total_ref[...] = add_far(total_ref[...], left, block_ref, at * rows, rank, dim)

        out_ref[...] = total_ref[...].astype(BF16)

    return call(
        kernel,
        shaped(rank, LANES),
        [(far_row, SMEM), (leaf_t, VMEM), (transfer, VMEM), (mine, VMEM), (got, VMEM)],
        scratch=[VMEM((rank, LANES), F32)],
        flops=2 * 8 * rank * rank * 512,
    )


def routed(block, axis, target):
    size = lax.axis_size(axis)
    route = [(i, target(i)) for i in range(size) if 0 <= target(i) < size]
    return lax.ppermute(block, axis, route)


def over_chips(i):
    return i + 2 - 4 * (i % 2)


def beside_chips(i):
    return i - 1 + 2 * (i % 2)


def on_chip(i):
    return i ^ 1


def body(
    points,
    ordering,
    iterate,
    target,
    step_size,
    leaf_basis,
    transfer,
    leaf_skeleton,
    cluster_skeleton,
    near_table,
    far_table,
    cluster_far,
):
    plan = Plan(points, iterate)
    leaves = lax.axis_size("leaf")
    groups = lax.axis_size("group")
    rank = leaf_basis.shape[1]
    leaf_t = jnp.swapaxes(leaf_skeleton, 1, 2)
    cluster_t = jnp.swapaxes(cluster_skeleton, 1, 2)

    pay, down_block, up_block = prepare(
        plan, near_table, iterate, points.T, leaf_basis, transfer, leaf_t, cluster_t
    )
    partner = routed(pay, "leaf", on_chip)
    over = routed(pay, "leaf", over_chips)
    others = [routed(up_block, "group", lambda i, k=k: i ^ k) for k in range(1, groups)]
    step_row = step_size.reshape(1, -1)
    acc, base = own_tile(plan, pay, ordering, target, iterate, step_row)
    mine = across(cluster_far, cluster_t, up_block, others, lambda me, k: me ^ (k + 1), down_block)
    acc, left, row = pair_tiles(plan, pay, partner, acc)

    xors, bit = [0], leaves // 2
    while True:
        got = routed(mine, "leaf", lambda i, bit=bit: i ^ bit)
        xors = xors + [x ^ bit for x in xors]
        if bit == 1:
            break
        mine = joined(mine, got, rank)
        bit //= 2
    local = down(far_table, leaf_t, transfer, mine, got, xors)

    beside = routed(pay, "leaf", beside_chips)
    over_passed = routed(over, "leaf", on_chip)
    (acc,) = side_tiles(plan, row, left, over, over_passed, acc, 2, False)
    beside_passed = routed(beside, "leaf", on_chip)
    third = routed(beside, "leaf", over_chips)
    acc, theirs = side_tiles(plan, row, left, beside, beside_passed, acc, 1, True)
    returned = routed(theirs, "leaf", on_chip)
    acc = third_tile(plan, row, left, third, acc)
    return finish(plan, pay, acc, returned, base, step_row, leaf_basis, local)


def solution(mesh):
    return jax.shard_map(
        body,
        mesh=mesh,
        in_specs=(
            P(("group", "leaf"), None),
            P(("group", "leaf"), None),
            P(("group", "leaf"), None),
            P(("group", "leaf"), None),
            P(),
            P(("group", "leaf"), None),
            P(("group", "leaf"), None, None),
            P(("group", "leaf"), None, None),
            P("group", None, None),
            P(("group", "leaf"), None),
            P(("group", "leaf"), None),
            P("group", None),
        ),
        out_specs=P(("group", "leaf"), None),
        check_vma=False,
    )
```

```python
import math

import jax
import jax.numpy as jnp
from jax import lax
from jax.experimental import pallas as pl
from jax.experimental.pallas import tpu as pltpu
from jax.sharding import PartitionSpec as P


LANES = 128
COLS = 256
ROWS = 1024
FLAG_ROWS = 16
SHIFT = 66.0
LOG2E = math.log2(math.e)
VMEM = pltpu.VMEM
SMEM = pltpu.SMEM
HBM = pltpu.HBM
F32 = jnp.float32
BF16 = jnp.bfloat16


def contract(left, right, dims):
    return lax.dot_general(left, right, (dims, ((), ())), preferred_element_type=F32)


def matmul(left, right):
    return contract(left, right, ((1,), (0,)))


def call(kernel, outs, ins, scratch=(), flops=0, limit=16, aliases=None, into=VMEM):
    single = not isinstance(outs, (list, tuple))
    shapes = [outs] if single else list(outs)
    results = pl.pallas_call(
        kernel,
        out_shape=shapes,
        in_specs=[pl.BlockSpec(memory_space=space) for _, space in ins],
        out_specs=[pl.BlockSpec(memory_space=into)] * len(shapes),
        scratch_shapes=list(scratch),
        input_output_aliases=aliases or {},
        compiler_params=pltpu.CompilerParams(vmem_limit_bytes=limit << 20),
        cost_estimate=pl.CostEstimate(
            flops=int(flops), bytes_accessed=sum(a.size * a.dtype.itemsize for a, _ in ins), transcendentals=0
        ),
    )(*[a for a, _ in ins])
    return results[0] if single else results


def shaped(*shape, dtype=BF16):
    return jax.ShapeDtypeStruct(shape, dtype)


class Plan:
    def __init__(self, points, iterate):
        self.n, self.dim = points.shape
        self.rhs = iterate.shape[1]
        self.half = self.n // 2
        self.blocks = self.half // LANES
        self.flags = self.half + self.blocks * self.dim
        self.rows = self.flags + FLAG_ROWS
        self.tile_flops = 2 * self.n * self.n * 512

    def pay(self):
        return shaped(2, self.rows, self.rhs)

    def acc(self):
        return shaped(2, self.n, self.rhs, dtype=F32)

    def left(self):
        return shaped(2, self.n, self.dim)

    def offset_scratch(self):
        return [VMEM((8, self.half), F32)]


def three_parts(value):
    high = value.astype(BF16).astype(F32)
    rest = value - high
    middle = rest.astype(BF16).astype(F32)
    return high, middle, rest - middle


def extended(doubled, left):
    dim, width = doubled.shape
    wide = doubled.astype(F32)
    parts = three_parts(-0.25 * jnp.sum(wide * wide, axis=0, keepdims=True))
    row = lax.broadcasted_iota(jnp.int32, (LANES - dim, width), 0)
    ones, first = (0, 3) if left else (3, 0)
    below = jnp.where((row >= ones) & (row < ones + 3), 1.0, 0.0)
    for k, part in enumerate(parts):
        below = jnp.where(row == first + k, part, below)
    return jnp.concatenate([0.5 * wide if left else wide, below], axis=0)


def small_left(doubled):
    width = doubled.shape[1]
    return jnp.concatenate(
        [extended(doubled[:, k : k + LANES], True).T.astype(BF16) for k in range(0, width, LANES)], axis=0
    )


def doubled_of(ref):
    return (2.0 * ref[0].astype(F32)).astype(BF16)


def left_block(doubled):
    twice = jnp.concatenate([doubled, doubled], axis=0).astype(F32)
    return (0.5 * twice.T)[:, 0 : doubled.shape[0]].astype(BF16)


def doubled_block(plan, ref, b):
    return ref[plan.half + b * plan.dim : plan.half + (b + 1) * plan.dim, :]


def fill_left(plan, out_ref, ref, h):
    for b in range(plan.blocks):
        first = h * plan.half + b * LANES
        out_ref[first : first + LANES, :] = left_block(doubled_block(plan, ref, b))


def norms(doubled):
    wide = doubled.astype(F32)
    return (0.25 * LOG2E) * jnp.sum(wide * wide, axis=0, keepdims=True)


def fill_offset(plan, offset_ref, ref):
    for b in range(plan.blocks):
        offset_ref[0:1, b * LANES : (b + 1) * LANES] = -norms(doubled_block(plan, ref, b)) - SHIFT


def half_tile(plan, acc_ref, left_ref, source_ref, offset_ref, beside=None):
    step = 0
    for r in range(0, plan.n, ROWS):
        left = left_ref[r : r + ROWS, :]
        total = acc_ref[r : r + ROWS, :]
        for c in range(0, plan.half, COLS):
            cols = slice(c, c + COLS)
            right = jnp.concatenate(
                [doubled_block(plan, source_ref, b) for b in range(c // LANES, (c + COLS) // LANES)], axis=1
            )
            power = matmul(left, right) * LOG2E + offset_ref[0:1, cols]
            total = total + matmul(jnp.exp2(power).astype(BF16), source_ref[cols, :])
            if beside is not None:
                beside(step)
            step += 1
        acc_ref[r : r + ROWS, :] = total


def pick(row, place):
    lane = lax.broadcasted_iota(jnp.int32, row.shape, 1)
    return jnp.sum(jnp.where(lane == place, row, 0.0)) > 0


def skeleton_rows(rank, dim):
    return (rank // LANES) * dim


def prepare(plan, near_row, iterate, points_t, basis, transfer, leaf_t, cluster_t):
    size = near_row.shape[1]
    n, half, dim = plan.n, plan.half, plan.dim
    rank = basis.shape[1]

    inputs = [points_t, iterate, near_row, leaf_t, cluster_t, basis, transfer]

    def kernel(*refs):
        count = len(inputs)
        sources, (pay_ref, down_ref, up_ref) = refs[:count], refs[count : count + 3]
        points_ref, iterate_ref, near_ref, leaf_ref, cluster_ref, basis_ref, transfer_ref, sems = refs[count + 3 :]
        copies = [
            pltpu.make_async_copy(source, into, sems.at[k])
            for k, (source, into) in enumerate(zip(sources, refs[count + 3 : -1]))
        ]
        for copy in copies:
            copy.start()
        copies[0].wait()
        for h in range(2):
            for b in range(plan.blocks):
                first = h * half + b * LANES
                pay_ref[h, half + b * dim : half + (b + 1) * dim, :] = (
                    2.0 * points_ref[:, first : first + LANES].astype(F32)
                ).astype(BF16)
        copies[1].wait()
        for h in range(2):
            pay_ref[h, 0:half, :] = iterate_ref[h * half : (h + 1) * half, :].astype(BF16)
        for copy in copies[2:]:
            copy.wait()
        lane = lax.broadcasted_iota(jnp.int32, (FLAG_ROWS, LANES), 1)
        row = jnp.zeros((FLAG_ROWS, LANES), F32)
        for k in range(size):
            row = jnp.where(lane == k, near_ref[0, k].astype(F32), row)
        for h in range(2):
            pay_ref[h, plan.flags :, :] = row.astype(BF16)

        def skeleton(ref, out_ref):
            doubled = doubled_of(ref)
            for b in range(rank // LANES):
                out_ref[rank + b * dim : rank + (b + 1) * dim, :] = doubled[:, b * LANES : (b + 1) * LANES]

        skeleton(leaf_ref, down_ref)
        skeleton(cluster_ref, up_ref)
        total = jnp.zeros((rank, plan.rhs), F32)
        for h in range(2):
            total = total + contract(
                basis_ref[h * half : (h + 1) * half, :], pay_ref[h, 0:half, :], ((0,), (0,))
            )
        coef = total.astype(BF16)
        down_ref[0:rank, :] = coef
        up_ref[0:rank, :] = contract(transfer_ref[0], coef, ((0,), (0,))).astype(BF16)

    rows = rank + skeleton_rows(rank, dim)
    return call(
        kernel,
        [plan.pay(), shaped(rows, plan.rhs), shaped(rows, plan.rhs)],
        [(pltpu.with_memory_space_constraint(value, HBM), HBM) for value in inputs],
        scratch=[(SMEM if value is near_row else VMEM)(value.shape, value.dtype) for value in inputs]
        + [pltpu.SemaphoreType.DMA((len(inputs),))],
        flops=2 * n * rank * plan.rhs,
    )


def own_tile(plan, pay, ordering, target, iterate, step_size):
    group = 8
    steps = (plan.n // ROWS) * (plan.half // COLS)
    rows = plan.half // steps

    def kernel(pay_ref, order_ref, target_ref, iterate_ref, step_ref, acc_ref, base_ref, left_ref, offset_ref):
        acc_ref[...] = jnp.zeros_like(acc_ref)
        for h in range(2):
            fill_left(plan, left_ref, pay_ref.at[h], h)
        step_row = step_ref[...]

        @pl.loop(0, 2)
        def _(h):
            def beside(step):
                for k in range(step * rows, (step + 1) * rows, group):
                    first = pl.multiple_of(h * plan.half + k, group)
                    here = pl.ds(first, group)
                    wanted = jnp.concatenate(
                        [target_ref[pl.ds(order_ref[0, first + u], 1), :] for u in range(group)], axis=0
                    )
                    base_ref[here, :] = iterate_ref[here, :] + step_row * wanted

            fill_offset(plan, offset_ref, pay_ref.at[h])
            half_tile(plan, acc_ref.at[0], left_ref, pay_ref.at[h], offset_ref, beside)

    full = shaped(plan.n, plan.rhs, dtype=F32)
    return call(
        kernel,
        [plan.acc(), full],
        [(pay, VMEM), (ordering, SMEM), (target, VMEM), (iterate, VMEM), (step_size, VMEM)],
        scratch=[VMEM(plan.left().shape[1:], BF16)] + plan.offset_scratch(),
        flops=plan.tile_flops,
    )


def pair_tiles(plan, pay, partner, acc):
    def kernel(pay_ref, partner_ref, acc_in, acc_ref, left_ref, row_ref, offset_ref):
        place = lax.axis_index("leaf")
        core = lax.rem(place, 2)
        for h in range(2):
            fill_left(plan, left_ref.at[0], pay_ref.at[h], h)
            fill_left(plan, left_ref.at[1], partner_ref.at[h], h)
        rows = [ref[0, plan.flags :, :].astype(F32) for ref in (pay_ref, partner_ref)]
        for t in range(2):
            row_ref[t] = rows[t][0:8, :]

        @pl.when(pick(rows[0][0:8, :], place + 1 - 2 * core))
        def _():
            fill_offset(plan, offset_ref, partner_ref.at[core])
            half_tile(plan, acc_ref.at[0], left_ref.at[0], partner_ref.at[core], offset_ref)

        @pl.when(pick(rows[1][0:8, :], place))
        def _():
            fill_offset(plan, offset_ref, pay_ref.at[core])
            half_tile(plan, acc_ref.at[1], left_ref.at[1], pay_ref.at[core], offset_ref)

    return call(
        kernel,
        [plan.acc(), plan.left(), shaped(2, 8, LANES, dtype=F32)],
        [(pay, VMEM), (partner, VMEM), (acc, VMEM)],
        scratch=plan.offset_scratch(),
        flops=plan.tile_flops,
        aliases={2: 0},
    )


def side_tiles(plan, row, left, full, passed, acc, reach):
    def kernel(row_ref, left_ref, full_ref, passed_ref, acc_in, acc_ref, *refs):
        offset_ref = refs[-1]
        place = lax.axis_index("leaf")
        core = lax.rem(place, 2)
        away = 2 * core - 1
        first = place + away * reach
        second = place - away - away * reach
        for source, at in ((full_ref.at[core], first), (passed_ref.at[core], second)):
            on_mine = pick(row_ref[0], at)
            on_theirs = pick(row_ref[1], at)

            @pl.when(on_mine | on_theirs)
            def _():
                fill_offset(plan, offset_ref, source)

            @pl.loop(0, 2)
            def _(t):
                @pl.when(jnp.where(t == 0, on_mine, on_theirs))
                def _():
                    half_tile(plan, acc_ref.at[t], left_ref.at[t], source, offset_ref)

    outs = plan.acc()
    return call(
        kernel,
        outs,
        [(row, VMEM), (left, VMEM), (full, VMEM), (passed, VMEM), (acc, VMEM)],
        scratch=plan.offset_scratch(),
        flops=2 * plan.tile_flops,
        aliases={4: 0},
    )


def third_tile(plan, row, left, third, passed, acc):
    def kernel(row_ref, left_ref, third_ref, passed_ref, acc_in, acc_ref, theirs_ref, offset_ref):
        place = lax.axis_index("leaf")
        core = lax.rem(place, 2)
        away = 2 * core - 1
        for t, source, at in ((0, third_ref.at[core], place + 3 * away), (1, passed_ref.at[core], place - 4 * away)):

            @pl.when(pick(row_ref[t], at))
            def _():
                fill_offset(plan, offset_ref, source)
                half_tile(plan, acc_ref.at[t], left_ref.at[t], source, offset_ref)

        theirs_ref[...] = acc_ref[1].astype(BF16)

    return call(
        kernel,
        [plan.acc(), shaped(plan.n, plan.rhs)],
        [(row, VMEM), (left, VMEM), (third, VMEM), (passed, VMEM), (acc, VMEM)],
        scratch=plan.offset_scratch(),
        flops=plan.tile_flops,
        aliases={4: 0},
    )


def finish(plan, pay, acc, returned, base, step_size, basis, local):
    piece = 4 * LANES

    def kernel(pay_ref, acc_ref, returned_ref, base_ref, step_ref, basis_ref, local_ref, out_hbm, out_ref, sems):
        copies = []
        for first in range(0, plan.n, piece):
            rows = slice(first, first + piece)
            far = matmul(basis_ref[rows, :], local_ref[...])
            near = acc_ref[0, rows, :] + returned_ref[rows, :].astype(F32)
            powers = [
                SHIFT - norms(doubled_block(plan, pay_ref.at[at // plan.half], at % plan.half // LANES))
                for at in range(first, first + piece, LANES)
            ]
            factor = jnp.concatenate([jnp.exp2(jnp.broadcast_to(p, (LANES, LANES)).T) for p in powers], axis=0)
            out_ref[rows, :] = base_ref[rows, :] - step_ref[...] * (far + factor * near)
            copies.append(pltpu.make_async_copy(out_ref.at[rows, :], out_hbm.at[rows, :], sems.at[len(copies)]))
            copies[-1].start()
        for copy in copies:
            copy.wait()

    return call(
        kernel,
        shaped(plan.n, plan.rhs, dtype=F32),
        [(value, VMEM) for value in (pay, acc, returned, base, step_size, basis, local)],
        scratch=[VMEM((plan.n, plan.rhs), F32), pltpu.SemaphoreType.DMA((plan.n // piece,))],
        into=HBM,
        flops=2 * plan.n * basis.shape[1] * plan.rhs,
    )


def add_far(total, left, block_ref, first, rank, dim):
    right = jnp.concatenate(
        [
            extended(block_ref[first + rank + b * dim : first + rank + (b + 1) * dim, :], False).astype(BF16)
            for b in range(rank // LANES)
        ],
        axis=1,
    )
    return total + matmul(jnp.exp(matmul(left, right)).astype(BF16), block_ref[first : first + rank, :])


def across(cluster_row, cluster_t, own, others, distances, down_block):
    dim, rank = cluster_t.shape[1:]
    count = len(others)
    rows = down_block.shape[0]

    def kernel(far_ref, skeleton_ref, down_ref, own_ref, *refs):
        out_ref, total_ref = refs[count], refs[count + 1]
        me = lax.axis_index("group")
        left = small_left(doubled_of(skeleton_ref))
        total_ref[...] = jnp.zeros_like(total_ref)
        out_ref[0:rows, :] = down_ref[...]

        def include(at, block_ref):
            @pl.when(far_ref[0, at] > 0)
            def _():
                total_ref[...] = add_far(total_ref[...], left, block_ref, 0, rank, dim)

        include(me, own_ref)
        for k in range(count):
            include(distances(me, k), refs[k])
        out_ref[rows:, :] = total_ref[...].astype(BF16)

    return call(
        kernel,
        shaped(rows + rank, LANES),
        [(cluster_row, SMEM), (cluster_t, VMEM), (down_block, VMEM), (own, VMEM)] + [(o, VMEM) for o in others],
        scratch=[VMEM((rank, LANES), F32)],
        flops=2 * 4 * rank * rank * 512,
    )


def joined(mine, got, rank):
    rows = mine.shape[0] - rank

    def kernel(mine_ref, got_ref, out_ref):
        out_ref[0:rows, :] = mine_ref[0:rows, :]
        out_ref[rows : 2 * rows, :] = got_ref[0:rows, :]
        out_ref[2 * rows :, :] = (mine_ref[rows:, :].astype(F32) + got_ref[rows:, :].astype(F32)).astype(BF16)

    return call(kernel, shaped(2 * rows + rank, LANES), [(mine, VMEM), (got, VMEM)])


def down(far_row, leaf_t, transfer, mine, got, xors):
    dim, rank = leaf_t.shape[1:]
    rows = rank + skeleton_rows(rank, dim)
    count = (mine.shape[0] - rank) // rows

    def kernel(far_ref, skeleton_ref, transfer_ref, mine_ref, got_ref, out_ref, total_ref):
        place = lax.axis_index("leaf")
        left = small_left(doubled_of(skeleton_ref))
        lower = (mine_ref[count * rows :, :].astype(F32) + got_ref[count * rows :, :].astype(F32)).astype(BF16)
        total_ref[...] = matmul(transfer_ref[0], lower)
        for k, other in enumerate(xors):
            block_ref, at = (mine_ref, k) if k < count else (got_ref, k - count)

            @pl.when(far_ref[0, place ^ other] > 0)
            def _():
                total_ref[...] = add_far(total_ref[...], left, block_ref, at * rows, rank, dim)

        out_ref[...] = total_ref[...].astype(BF16)

    return call(
        kernel,
        shaped(rank, LANES),
        [(far_row, SMEM), (leaf_t, VMEM), (transfer, VMEM), (mine, VMEM), (got, VMEM)],
        scratch=[VMEM((rank, LANES), F32)],
        flops=2 * 8 * rank * rank * 512,
    )


def routed(block, axis, target):
    size = lax.axis_size(axis)
    route = [(i, target(i)) for i in range(size) if 0 <= target(i) < size]
    return lax.ppermute(block, axis, route)


def over_chips(i):
    return i + 2 - 4 * (i % 2)


def beside_chips(i):
    return i - 1 + 2 * (i % 2)


def on_chip(i):
    return i ^ 1


def body(
    points,
    ordering,
    iterate,
    target,
    step_size,
    leaf_basis,
    transfer,
    leaf_skeleton,
    cluster_skeleton,
    near_table,
    far_table,
    cluster_far,
):
    plan = Plan(points, iterate)
    leaves = lax.axis_size("leaf")
    groups = lax.axis_size("group")
    rank = leaf_basis.shape[1]
    leaf_t = jnp.swapaxes(leaf_skeleton, 1, 2)
    cluster_t = jnp.swapaxes(cluster_skeleton, 1, 2)

    pay, down_block, up_block = prepare(
        plan, near_table, iterate, points.T, leaf_basis, transfer, leaf_t, cluster_t
    )
    partner = routed(pay, "leaf", on_chip)
    over = routed(pay, "leaf", over_chips)
    others = [routed(up_block, "group", lambda i, k=k: i ^ k) for k in range(1, groups)]
    step_row = step_size.reshape(1, -1)
    acc, base = own_tile(plan, pay, ordering, target, iterate, step_row)
    mine = across(cluster_far, cluster_t, up_block, others, lambda me, k: me ^ (k + 1), down_block)
    acc, left, row = pair_tiles(plan, pay, partner, acc)

    xors, bit = [0], leaves // 2
    while True:
        got = routed(mine, "leaf", lambda i, bit=bit: i ^ bit)
        xors = xors + [x ^ bit for x in xors]
        if bit == 1:
            break
        mine = joined(mine, got, rank)
        bit //= 2
    local = down(far_table, leaf_t, transfer, mine, got, xors)

    beside = routed(pay, "leaf", beside_chips)
    over_passed = routed(over, "leaf", on_chip)
    acc = side_tiles(plan, row, left, over, over_passed, acc, 2)
    beside_passed = routed(beside, "leaf", on_chip)
    third = routed(beside, "leaf", over_chips)
    acc = side_tiles(plan, row, left, beside, beside_passed, acc, 1)
    third_passed = routed(third, "leaf", on_chip)
    acc, theirs = third_tile(plan, row, left, third, third_passed, acc)
    returned = routed(theirs, "leaf", on_chip)
    return finish(plan, pay, acc, returned, base, step_row, leaf_basis, local)


def solution(mesh):
    return jax.shard_map(
        body,
        mesh=mesh,
        in_specs=(
            P(("group", "leaf"), None),
            P(("group", "leaf"), None),
            P(("group", "leaf"), None),
            P(("group", "leaf"), None),
            P(),
            P(("group", "leaf"), None),
            P(("group", "leaf"), None, None),
            P(("group", "leaf"), None, None),
            P("group", None, None),
            P(("group", "leaf"), None),
            P(("group", "leaf"), None),
            P("group", None),
        ),
        out_specs=P(("group", "leaf"), None),
        check_vma=False,
    )
```
